256 devices in a mesh: blk: 64 (over z, x, core), rep: 4 (over y).
Axes of the slice: x: 4, y: 4, z: 8, core: 2. Of those that a mesh axis runs over, the one named last changes fastest.
Arguments:
- amplitudes: float32 [64, 64, 16, 512], P('blk', None, 'rep'), may hold values from -6 to 6
- cycle_integrals: float32 [32, 64, 64, 512], P('rep', None, 'blk'), may hold values from -0.09375 to 0.09375
- cross_integrals: float32 [32, 64, 64, 512], P('rep', None, 'blk'), may hold values from -0.09375 to 0.09375
- occ_energy: float32 [64], replicated, may hold values from -2 to -0.5
- vir_energy_a: float32 [32], replicated, may hold values from 0.2 to 3
- vir_energy_b: float32 [16], replicated, may hold values from 0.2 to 3
Outputs:
- update: float32 [64, 32, 16, 64], P('blk', 'rep')
- residual_rms: float32 [], replicated
The draws below stay inside these ranges and needn't reach their ends.
All inputs are finite; a program needn't handle non-finite values.
Results may differ from the reference program's by a relative error of at most 0.0006.
Values sent between devices are 32-bit elements; how exact they have to be, the bound alone decides.
A program may use at most 64 MiB of HBM per device.

```python
import jax
import jax.numpy as jnp
from jax import lax

O = 64
V = 512
A = 32
B = 16


def raised(drawn, rng, source, target, parts, factor):
    def block_of(axis_at):
        return (jnp.arange(drawn.shape[axis_at]) // (drawn.shape[axis_at] // parts)).reshape((-1,) + (1,) * (drawn.ndim - 1 - axis_at))

    near = jax.random.permutation(rng, parts)[block_of(target)]
    second = (block_of(target) + parts // 2) % parts
    return jnp.where((block_of(source) == near) | (block_of(source) == second), factor * drawn, drawn)


def shard_levels(rng, extent, split, low, largest):
    loudness, own = 1.0, jax.random.fold_in(rng, 6)
    for dim, parts in split:
        heights = jnp.exp(jax.random.uniform(jax.random.fold_in(own, dim), (parts,), jnp.float32, low / len(split), largest / len(split)))
        loudness = loudness * jnp.repeat(heights, extent[dim] // parts).reshape([-1 if axis == dim else 1 for axis in range(len(extent))])
    return loudness


def gaussian(own_key, extent, width, limit, cuts=(), dtype=jnp.bfloat16):
    array = jax.random.normal(own_key, extent, jnp.float32) * width
    if len(cuts) > 0:
        array = shard_levels(own_key, extent, cuts, -0.22, 0.18) * array
    return jnp.clip(array, min=-limit, max=limit).astype(dtype)


def bell_draw_with(key, dims, spread, reach, cuts, heavy, kind=jnp.bfloat16):
    array = spread * jax.random.normal(key, dims, jnp.float32)
    if cuts:
        array = array * shard_levels(key, dims, cuts, -0.22, 0.18)
    return jnp.clip(raised(array, jax.random.fold_in(key, 3), *heavy), -reach, reach).astype(kind)


def setup_inputs(seed: int = 0) -> dict:
    key_of = jax.random.split(jax.random.key(seed), 7)
    amplitudes = gaussian(key_of[0], (O, O, B, V), 1.0, 6.0, ((0, 64), (2, 4)), jnp.float32)
    cycle_integrals = bell_draw_with(key_of[1], (A, O, O, V), (O * V) ** -0.5, 0.09375, ((0, 4), (2, 64)), (2, 1, 64, 4.0), jnp.float32)
    cross_integrals = bell_draw_with(key_of[2], (A, O, O, V), (O * V) ** -0.5, 0.09375, ((0, 4), (2, 64)), (2, 1, 64, 4.0), jnp.float32)
    occ_energy = jnp.clip(jax.random.uniform(key_of[3], (O,), jnp.float32, -2.0, -0.5), -2.0, -0.5)
    vir_energy_a = jnp.clip(jax.random.uniform(key_of[4], (A,), jnp.float32, 0.2, 3.0), 0.2, 3.0)
    vir_energy_b = jnp.clip(jax.random.uniform(key_of[5], (B,), jnp.float32, 0.2, 3.0), 0.2, 3.0)
    return dict(amplitudes=amplitudes, cycle_integrals=cycle_integrals, cross_integrals=cross_integrals, occ_energy=occ_energy, vir_energy_a=vir_energy_a, vir_energy_b=vir_energy_b)


def reference(amplitudes, cycle_integrals, cross_integrals, occ_energy, vir_energy_a, vir_energy_b):
    highest = lax.Precision.HIGHEST
    cycle = jnp.einsum('aikc,kjbc->iabj', cycle_integrals, amplitudes, precision=highest)
    cross = jnp.einsum('aikc,jkbc->iabj', cross_integrals, amplitudes, precision=highest)
    residual = cycle + cross
    denom = occ_energy[:, None, None, None] + occ_energy[None, None, None, :] - vir_energy_a[None, :, None, None] - vir_energy_b[None, None, :, None]
    update = residual / denom
    residual_rms = jnp.sqrt(jnp.sum(residual * residual) / (O * A * B * O))
    return (update, residual_rms)
```

```python
import functools

import jax
import jax.numpy as jnp
from jax import lax
from jax.experimental import pallas as pl
from jax.experimental.pallas import tpu as pltpu
from jax.sharding import PartitionSpec as P

MESH = pl.DeviceIdType.MESH
F32 = jnp.float32
BF16 = jnp.bfloat16
NY = 4
NB = 4
NA = 8
NC = 512
CT = NC // 128
ROWS = NB * CT
KT = 3 * NC


def ring_order(n):
    order = [0]
    for d in range(1, n // 2 + 1):
        order.append(d)
        if n - d != d:
            order.append(n - d)
    return order


def kernel(
    nz, nx,
    t_hbm, w_hbm, x_hbm, res_ref, rms_ref,
    tb, tt, a1, wv, xv, wop, top, part, ra, s1, rb, s2, rc, ssz, ssx, ssy,
    load_sem, ty_send, ty_recv, tf_send, tf_recv, z_send, z_recv, c_send, c_recv, c_loc,
    tty_send, tty_recv, ttf_send, ttf_recv, ra_send, ra_recv, rb_send, rb_recv, rc_send, rc_recv,
    ss_send, ss_recv,
):
    nxc = nx * 2
    no = nz * nxc
    blk_rows = no * ROWS
    me, y = lax.axis_index("blk"), lax.axis_index("rep")
    z, xc = me // nxc, me % nxc
    x, core = xc // 2, xc % 2
    up, down, far = (y + 1) % NY, (y + NY - 1) % NY, (y + 2) % NY
    order = ring_order(nz)

    def at_y(yy):
        return {"blk": me, "rep": yy}

    def at_blk(b):
        return {"blk": b, "rep": y}

    def zpeer(d):
        return (z + d) % nz

    def xcpeer(d):
        return (xc + d) % nxc

    def send(src, dst, ssem, rsem, dev):
        pltpu.make_async_remote_copy(
            src_ref=src, dst_ref=dst, send_sem=ssem, recv_sem=rsem, device_id=dev, device_id_type=MESH
        ).start()

    def arrived(ref, sem):
        pltpu.make_async_copy(ref, ref, sem).wait()

    def rows(start, n):
        return pl.ds(pl.multiple_of(start, ROWS), n)

    barrier = pltpu.get_barrier_semaphore()
    count = 0
    for d in range(1, nz):
        pl.semaphore_signal(barrier, inc=1, device_id=at_blk(zpeer(d) * nxc + xc), device_id_type=MESH)
        count += 1
    for d in range(1, nxc):
        pl.semaphore_signal(barrier, inc=1, device_id=at_blk(z * nxc + xcpeer(d)), device_id_type=MESH)
        count += 1
    for yy in (up, down, far):
        pl.semaphore_signal(barrier, inc=1, device_id=at_y(yy), device_id_type=MESH)
        count += 1
    pl.semaphore_wait(barrier, count)

    half = blk_rows // 2
    mine = y * blk_rows

    for h in (0, 1):
        send(t_hbm.at[rows(h * half, half)], tb.at[rows(mine + h * half, half)],
             ty_send, ty_recv.at[0, h], at_y(up))
        g = 1 - h
        send(t_hbm.at[rows(g * half, half)], tb.at[rows(mine + g * half, half)],
             ty_send, ty_recv.at[1, g], at_y(down))

    zrows = nxc * ROWS
    for d in order[1:]:
        zp = zpeer(d)
        send(t_hbm.at[rows(zp * zrows, zrows)], a1.at[rows(z * zrows, zrows)],
             z_send, z_recv.at[z], at_blk(zp * nxc + xc))

    def second_stage(src, zs):
        for d in range(1, nxc):
            p = xcpeer(d)
            send(src.at[rows(zs * zrows + p * ROWS, ROWS)], tt.at[rows(mine + zs * zrows + xc * ROWS, ROWS)],
                 c_send, c_recv.at[zs], at_blk(z * nxc + p))
        pltpu.make_async_copy(
            src.at[rows(zs * zrows + xc * ROWS, ROWS)], tt.at[rows(mine + zs * zrows + xc * ROWS, ROWS)],
            c_loc.at[zs]).start()

    second_stage(t_hbm, z)
    load_w = pltpu.make_async_copy(w_hbm, wv.at[pl.ds(0, NA * no * CT)], load_sem.at[0])
    load_x = pltpu.make_async_copy(x_hbm, xv.at[pl.ds(0, NA * no * CT)], load_sem.at[1])
    load_t = pltpu.make_async_copy(t_hbm, tb.at[rows(mine, blk_rows)], load_sem.at[2])
    load_w.start()
    load_x.start()
    load_t.start()

    def split(v):
        hi = v.astype(BF16)
        return hi, (v - hi.astype(F32)).astype(BF16)

    def prep_integrals(src, term):
        stride = no * CT

        def step(i2, carry):
            out = pl.ds(pl.multiple_of(i2 * 16, 16), 16)
            for ct in range(CT):
                v = jnp.concatenate(
                    [src[pl.ds((i2 * 2 + e) * CT + ct, NA, stride=stride), :] for e in range(2)], axis=0)
                hi, lo = split(v)
                base = term * KT + ct * 128
                wop[out, base:base + 128] = hi
                wop[out, base + NC:base + NC + 128] = lo
                wop[out, base + 2 * NC:base + 2 * NC + 128] = hi
            return carry

        lax.fori_loop(0, no // 2, step, 0)

    def prep_amplitudes(src, yb, term):
        def step(b, carry):
            out = pl.ds(pl.multiple_of(b * no, no), no)
            for ct in range(CT):
                v = src[pl.ds(yb * blk_rows + ct * NB + b, no, stride=ROWS), :]
                hi, lo = split(v)
                base = term * KT + ct * 128
                top[out, base:base + 128] = hi
                top[out, base + NC:base + NC + 128] = hi
                top[out, base + 2 * NC:base + 2 * NC + 128] = lo
            return carry

        lax.fori_loop(0, NB, step, 0)

    def multiply(slot, term):
        def step(kk, carry):
            cols = pl.ds(pl.multiple_of(term * KT + kk * NC, NC), NC)
            p = lax.dot_general(
                wop[:, cols], top[:, cols], (((1,), (1,)), ((), ())), preferred_element_type=F32)
            part[slot] += p.reshape(nz * nx, 2, NA, NB * no)
            return carry

        lax.fori_loop(0, KT // NC, step, 0)

    def cycle_term(slot, yb):
        part[slot] = jnp.zeros(part.shape[1:], F32)
        prep_amplitudes(tb, yb, 0)
        multiply(slot, 0)

    def cross_term(slot, yb):
        prep_amplitudes(tt, yb, 1)
        multiply(slot, 1)

    def core_stage(slot):
        send(part.at[slot, :, 1 - core], ra.at[slot], ra_send, ra_recv.at[slot], at_blk(z * nxc + x * 2 + 1 - core))

    def x_stage(slot):
        arrived(ra.at[slot], ra_recv.at[slot])
        s1[slot] = (part[slot, :, core] + ra[slot]).reshape(nz, nx, NA, NB * no)
        for d in range(1, nx):
            p = (x + d) % nx
            send(s1.at[slot, :, p], rb.at[slot, d - 1], rb_send, rb_recv.at[slot], at_blk(z * nxc + p * 2 + core))

    def z_stage(slot):
        arrived(rb.at[slot], rb_recv.at[slot])
        total = s1[slot, :, x]
        for d in range(nx - 1):
            total = total + rb[slot, d]
        s2[slot] = total
        for d in range(1, nz):
            p = zpeer(d)
            send(s2.at[slot, p], rc.at[slot, d - 1], rc_send, rc_recv.at[slot], at_blk(p * nxc + xc))

    def final(slot, yb):
        arrived(rc.at[slot], rc_recv.at[slot])
        total = s2[slot, z]
        for d in range(nz - 1):
            total = total + rc[slot, d]
        res_ref[:, pl.ds(pl.multiple_of(yb * NB * no, NB * no), NB * no)] = total
        sq = total * total
        if NB * no < 128:
            sq = jnp.concatenate([sq, jnp.zeros((NA, 128 - NB * no), F32)], axis=1)
        out = sq[:, 0:128]
        for n in range(1, NB * no // 128):
            out = out + sq[:, n * 128:(n + 1) * 128]
        return out

    def relay_stage(d):
        zs = (z + d) % nz
        arrived(a1.at[rows(zs * zrows, zrows)], z_recv.at[zs])
        second_stage(a1, zs)

    load_w.wait()
    prep_integrals(wv, 0)
    for d in order[1:3]:
        relay_stage(d)
    first = tb.at[rows(down * blk_rows, half)]
    arrived(first, ty_recv.at[0, 0])
    send(first, first, tf_send, tf_recv.at[0], at_y(up))
    second = tb.at[rows(up * blk_rows + half, half)]
    arrived(second, ty_recv.at[1, 1])
    send(second, second, tf_send, tf_recv.at[1], at_y(down))
    load_x.wait()
    prep_integrals(xv, 1)
    for d in order[3:]:
        relay_stage(d)

    for q, d in enumerate(order):
        zs = (z + d) % nz
        arrived(tt.at[rows(mine + zs * zrows, zrows - ROWS)], c_recv.at[zs])
        arrived(tt.at[rows(mine + zs * zrows, ROWS)], c_loc.at[zs])
        chunk = tt.at[rows(mine + zs * zrows, zrows)]
        send(chunk, chunk, tty_send, tty_recv.at[0, q], at_y(up))
        send(chunk, chunk, tty_send, tty_recv.at[1, q], at_y(down))

    load_t.wait()
    cycle_term(0, y)
    cross_term(0, y)
    core_stage(0)

    def forward(q):
        zs = (z + order[q]) % nz
        way = q % 2
        src_y, dst_y = ((down, up), (up, down))[way]
        chunk = tt.at[rows(src_y * blk_rows + zs * zrows, zrows)]
        arrived(chunk, tty_recv.at[way, q])
        send(chunk, chunk, ttf_send, ttf_recv.at[q], at_y(dst_y))

    for q in range(nz // 2):
        forward(q)
    arrived(tb.at[rows(down * blk_rows + half, half)], ty_recv.at[0, 1])
    cycle_term(1, down)
    x_stage(0)
    for q in range(nz // 2, nz):
        forward(q)
    for q, d in enumerate(order):
        if q % 2 == 1:
            zs = (z + d) % nz
            arrived(tt.at[rows(down * blk_rows + zs * zrows, zrows)], tty_recv.at[0, q])
    cross_term(1, down)
    core_stage(1)
    z_stage(0)
    arrived(tb.at[rows(up * blk_rows, half)], ty_recv.at[1, 0])
    cycle_term(2, up)
    for q, d in enumerate(order):
        if q % 2 == 0:
            zs = (z + d) % nz
            arrived(tt.at[rows(up * blk_rows + zs * zrows, zrows)], tty_recv.at[1, q])
    cross_term(2, up)
    core_stage(2)
    x_stage(1)
    arrived(tb.at[rows(far * blk_rows, half)], tf_recv.at[0])
    arrived(tb.at[rows(far * blk_rows + half, half)], tf_recv.at[1])
    cycle_term(3, far)
    x_stage(2)
    ss = final(0, y)
    for q, d in enumerate(order):
        zs = (z + d) % nz
        arrived(tt.at[rows(far * blk_rows + zs * zrows, zrows)], ttf_recv.at[q])
    cross_term(3, far)
    core_stage(3)
    z_stage(1)
    z_stage(2)
    x_stage(3)
    ss = ss + final(1, down)
    ss = ss + final(2, up)
    z_stage(3)
    ss = ss + final(3, far)

    def add_slots(ref, n):
        total = ref[0]
        for k in range(1, n):
            total = total + ref[k]
        return total

    ssz[z] = ss
    for d in range(1, nz):
        send(ssz.at[z], ssz.at[z], ss_send.at[0], ss_recv.at[0], at_blk(zpeer(d) * nxc + xc))
    arrived(ssz.at[pl.ds(0, nz - 1)], ss_recv.at[0])
    ssx[xc] = add_slots(ssz, nz)
    for d in range(1, nxc):
        send(ssx.at[xc], ssx.at[xc], ss_send.at[1], ss_recv.at[1], at_blk(z * nxc + xcpeer(d)))
    arrived(ssx.at[pl.ds(0, nxc - 1)], ss_recv.at[1])
    ssy[y] = add_slots(ssx, nxc)
    for yy in (up, down, far):
        send(ssy.at[y], ssy.at[y], ss_send.at[2], ss_recv.at[2], at_y(yy))
    arrived(ssy.at[pl.ds(0, NY - 1)], ss_recv.at[2])
    total = jnp.sum(add_slots(ssy, NY), keepdims=True)
    size = no * no * NA * NY * NB * NY
    rms_ref[...] = jnp.broadcast_to(jnp.sqrt(total / size), rms_ref.shape)

    arrived(tb.at[rows(0, 2 * blk_rows)], ty_send)
    arrived(tb.at[rows(0, blk_rows)], tf_send)
    arrived(a1.at[rows(0, (nz - 1) * zrows)], z_send)
    arrived(tt.at[rows(0, nz * (nxc - 1) * ROWS)], c_send)
    arrived(tt.at[rows(0, 2 * blk_rows)], tty_send)
    arrived(tt.at[rows(0, blk_rows)], ttf_send)
    arrived(ra, ra_send)
    if nx > 1:
        arrived(rb, rb_send)
    arrived(rc, rc_send)
    arrived(ssz.at[pl.ds(0, nz - 1)], ss_send.at[0])
    arrived(ssx.at[pl.ds(0, nxc - 1)], ss_send.at[1])
    arrived(ssy.at[pl.ds(0, NY - 1)], ss_send.at[2])


def residual_parts(nz, nx, t, w, x):
    nxc = nx * 2
    no = nz * nxc
    n = NB * no
    dma = pltpu.SemaphoreType.DMA
    return pl.pallas_call(
        functools.partial(kernel, nz, nx),
        out_shape=(jax.ShapeDtypeStruct((NA, NY * n), F32), jax.ShapeDtypeStruct((8, 128), F32)),
        in_specs=[pl.BlockSpec(memory_space=pl.ANY)] * 3,
        out_specs=(pl.BlockSpec(memory_space=pltpu.VMEM), pl.BlockSpec(memory_space=pltpu.VMEM)),
        scratch_shapes=[
            pltpu.VMEM((NY * no * ROWS + ROWS, 128), F32),
            pltpu.VMEM((NY * no * ROWS + ROWS, 128), F32),
            pltpu.VMEM((no * ROWS, 128), F32),
            pltpu.VMEM(((NA + 1) * no * CT, 128), F32),
            pltpu.VMEM(((NA + 1) * no * CT, 128), F32),
            pltpu.VMEM((NA * no, 2 * KT), BF16),
            pltpu.VMEM((n, 2 * KT), BF16),
            pltpu.VMEM((NY, nz * nx, 2, NA, n), F32),
            pltpu.VMEM((NY, nz * nx, NA, n), F32),
            pltpu.VMEM((NY, nz, nx, NA, n), F32),
            pltpu.VMEM((NY, max(nx - 1, 1), nz, NA, n), F32),
            pltpu.VMEM((NY, nz, NA, n), F32),
            pltpu.VMEM((NY, nz - 1, NA, n), F32),
            pltpu.VMEM((nz, 8, 128), F32),
            pltpu.VMEM((nxc, 8, 128), F32),
            pltpu.VMEM((NY, 8, 128), F32),
            dma((3,)),
            dma, dma((2, 2)), dma, dma((2,)),
            dma, dma((nz,)), dma, dma((nz,)), dma((nz,)),
            dma, dma((2, nz)), dma, dma((nz,)),
            dma, dma((NY,)), dma, dma((NY,)), dma, dma((NY,)),
            dma((3,)), dma((3,)),
        ],
        compiler_params=pltpu.CompilerParams(collective_id=0, has_side_effects=True),
    )(t, w, x)


def per_device(nz, nx, amplitudes, cycle_integrals, cross_integrals, occ_energy, vir_energy_a, vir_energy_b):
    no = nz * nx * 2
    t = amplitudes.reshape(no, NB, CT, 128).transpose(0, 2, 1, 3).reshape(no * ROWS, 128)
    w = cycle_integrals.reshape(NA * no * CT, 128)
    x = cross_integrals.reshape(NA * no * CT, 128)
    res, rms = residual_parts(nz, nx, t, w, x)
    residual = res.reshape(1, NA, NB * NY, no)
    occ_local = lax.dynamic_slice_in_dim(occ_energy, lax.axis_index("blk"), 1, 0)
    vir_local = lax.dynamic_slice_in_dim(vir_energy_a, lax.axis_index("rep") * NA, NA, 0)
    denom = (
        occ_local[:, None, None, None]
        + occ_energy[None, None, None, :]
        - vir_local[None, :, None, None]
        - vir_energy_b[None, None, :, None]
    )
    return residual / denom, rms[0, 0]


def solution(mesh, nz=8, nx=4):
    return jax.shard_map(
        functools.partial(per_device, nz, nx),
        mesh=mesh,
        in_specs=(
            P("blk", None, "rep", None),
            P("rep", None, "blk", None),
            P("rep", None, "blk", None),
            P(),
            P(),
            P(),
        ),
        out_specs=(P("blk", "rep", None, None), P()),
        check_vma=False,
    )
```

```python
import functools

import jax
import jax.numpy as jnp
from jax import lax
from jax.experimental import pallas as pl
from jax.experimental.pallas import tpu as pltpu
from jax.sharding import PartitionSpec as P

MESH = pl.DeviceIdType.MESH
F32 = jnp.float32
BF16 = jnp.bfloat16
NY = 4
NB = 4
NA = 8
NC = 512
CT = NC // 128
ROWS = NB * CT
KT = 3 * NC


def ring_order(n):
    order = [0]
    for d in range(1, n // 2 + 1):
        order.append(d)
        if n - d != d:
            order.append(n - d)
    return order


def kernel(
    nz, nx,
    t_hbm, w_hbm, x_hbm, occ_hbm, va_hbm, vb_hbm, upd_ref, rms_ref,
    tb, tt, a1, wv, xv, occ_v, va_v, vb_v, den, wop, top, part, ra, s1, rx, rb, rd, s2, rc, ssz, ssp,
    load_sem, ty_send, ty_recv, tf_send, tf_recv, z_send, z_recv, c_send, c_recv, c_loc,
    tty_send, tty_recv, ttf_send, ttf_recv, ra_send, ra_recv, rx_send, rx_recv, rb_send, rb_recv, rd_send, rd_recv, rc_send, rc_recv,
    ss_send, ss_recv,
):
    nxc = nx * 2
    no = nz * nxc
    blk_rows = no * ROWS
    hj = no // 2
    pc = NB * hj
    me, y = lax.axis_index("blk"), lax.axis_index("rep")
    z, xc = me // nxc, me % nxc
    x, core = xc // 2, xc % 2
    up, down, far = (y + 1) % NY, (y + NY - 1) % NY, (y + 2) % NY
    right, left, across = (x + 1) % nx, (x + nx - 1) % nx, (x + 2) % nx
    slot_y = (y, down, up, far)
    order = ring_order(nz)

    def at_y(yy):
        return {"blk": me, "rep": yy}

    def at_blk(b):
        return {"blk": b, "rep": y}

    def zpeer(d):
        return (z + d) % nz

    def xcpeer(d):
        return (xc + d) % nxc

    def send(src, dst, ssem, rsem, dev):
        pltpu.make_async_remote_copy(
            src_ref=src, dst_ref=dst, send_sem=ssem, recv_sem=rsem, device_id=dev, device_id_type=MESH
        ).start()

    def arrived(ref, sem):
        pltpu.make_async_copy(ref, ref, sem).wait()

    def rows(start, n):
        return pl.ds(pl.multiple_of(start, ROWS), n)

    barrier = pltpu.get_barrier_semaphore()
    count = 0
    for d in range(1, nz):
        pl.semaphore_signal(barrier, inc=1, device_id=at_blk(zpeer(d) * nxc + xc), device_id_type=MESH)
        count += 1

    def plane_peers():
        for e in (1, NY - 1, 0, 2):
            for d in range(nxc):
                if d or e:
                    yield {"blk": z * nxc + xcpeer(d), "rep": (y + e) % NY}

    for peer in plane_peers():
        pl.semaphore_signal(barrier, inc=1, device_id=peer, device_id_type=MESH)
        count += 1
    pl.semaphore_wait(barrier, count)

    half = blk_rows // 2
    mine = y * blk_rows

    for h in (0, 1):
        send(t_hbm.at[rows(h * half, half)], tb.at[rows(mine + h * half, half)],
             ty_send, ty_recv.at[0, h], at_y(up))
        g = 1 - h
        send(t_hbm.at[rows(g * half, half)], tb.at[rows(mine + g * half, half)],
             ty_send, ty_recv.at[1, g], at_y(down))

    zrows = nxc * ROWS
    for d in order[1:]:
        zp = zpeer(d)
        send(t_hbm.at[rows(zp * zrows, zrows)], a1.at[rows(z * zrows, zrows)],
             z_send, z_recv.at[z], at_blk(zp * nxc + xc))

    def second_stage(src, zs):
        for d in range(1, nxc):
            p = xcpeer(d)
            send(src.at[rows(zs * zrows + p * ROWS, ROWS)], tt.at[rows(mine + zs * zrows + xc * ROWS, ROWS)],
                 c_send, c_recv.at[zs], at_blk(z * nxc + p))
        pltpu.make_async_copy(
            src.at[rows(zs * zrows + xc * ROWS, ROWS)], tt.at[rows(mine + zs * zrows + xc * ROWS, ROWS)],
            c_loc.at[zs]).start()

    second_stage(t_hbm, z)
    load_w = pltpu.make_async_copy(w_hbm, wv.at[pl.ds(0, NA * no * CT)], load_sem.at[0])
    load_x = pltpu.make_async_copy(x_hbm, xv.at[pl.ds(0, NA * no * CT)], load_sem.at[1])
    load_t = pltpu.make_async_copy(t_hbm, tb.at[rows(mine, blk_rows)], load_sem.at[2])
    load_w.start()
    load_x.start()
    load_t.start()
    load_e = [
        pltpu.make_async_copy(src, dst, load_sem.at[3 + k])
        for k, (src, dst) in enumerate(((occ_hbm, occ_v), (va_hbm, va_v), (vb_hbm, vb_v)))
    ]
    for copy in load_e:
        copy.start()

    def split(v):
        hi = v.astype(BF16)
        return hi, (v - hi.astype(F32)).astype(BF16)

    def prep_integrals(src, term):
        stride = no * CT

        def step(i2, carry):
            out = pl.ds(pl.multiple_of(i2 * 16, 16), 16)
            for ct in range(CT):
                v = jnp.concatenate(
                    [src[pl.ds((i2 * 2 + e) * CT + ct, NA, stride=stride), :] for e in range(2)], axis=0)
                hi, lo = split(v)
                base = term * KT + ct * 128
                wop[out, base:base + 128] = hi
                wop[out, base + NC:base + NC + 128] = lo
                wop[out, base + 2 * NC:base + 2 * NC + 128] = hi
            return carry

        lax.fori_loop(0, no // 2, step, 0)

    def prep_amplitudes(src, yb, term, h):
        def step(b, carry):
            out = pl.ds(pl.multiple_of(h * pc + b * hj, hj), hj)
            for ct in range(CT):
                v = src[pl.ds(yb * blk_rows + h * hj * ROWS + ct * NB + b, hj, stride=ROWS), :]
                hi, lo = split(v)
                base = term * KT + ct * 128
                top[out, base:base + 128] = hi
                top[out, base + NC:base + NC + 128] = hi
                top[out, base + 2 * NC:base + 2 * NC + 128] = lo
            return carry

        lax.fori_loop(0, NB, step, 0)

    def product(term, kk, r):
        cols = pl.ds(pl.multiple_of(term * KT + kk * NC, NC), NC)
        p = lax.dot_general(wop[:, cols], top[r, cols], (((1,), (1,)), ((), ())), preferred_element_type=F32)
        return p.reshape(nz * nx, 2, NA, p.shape[1])

    def cycle_term(slot):
        for h in (0, 1):
            prep_amplitudes(tb, slot_y[slot], 0, h)
        part[slot] = product(0, 0, slice(None))

        def step(kk, carry):
            part[slot] += product(0, kk, slice(None))
            return carry

        lax.fori_loop(1, KT // NC, step, 0)

    def cross_term(slot, h):
        prep_amplitudes(tt, slot_y[slot], 1, h)
        c = slice(h * pc, (h + 1) * pc)

        def step(kk, carry):
            part[slot, :, :, :, c] += product(1, kk, c)
            return carry

        lax.fori_loop(0, KT // NC, step, 0)

    def core_stage(slot, h):
        c = slice(h * pc, (h + 1) * pc)
        n = slot * 2 + h
        send(part.at[slot, :, 1 - core, :, c], ra.at[n], ra_send, ra_recv.at[n], at_blk(z * nxc + x * 2 + 1 - core))

    hz = nz // 2

    def x_stage1(slot, h):
        c = slice(h * pc, (h + 1) * pc)
        n = slot * 2 + h
        arrived(ra.at[n], ra_recv.at[n])
        s1[n] = (part[slot, :, core, :, c] + ra[n]).reshape(nz, nx, NA, pc)
        send(s1.at[n, 0:hz, across], rx.at[n, 0], rx_send, rx_recv.at[n, 0], at_blk(z * nxc + right * 2 + core))
        send(s1.at[n, hz:nz, across], rx.at[n, 1], rx_send, rx_recv.at[n, 1], at_blk(z * nxc + left * 2 + core))

    def x_stage2(slot, h):
        n = slot * 2 + h
        arrived(rx.at[n, 0], rx_recv.at[n, 0])
        s1[n, 0:hz, right] += rx[n, 0]
        send(s1.at[n, :, right], rb.at[n, 0], rb_send, rb_recv.at[n, 0], at_blk(z * nxc + right * 2 + core))
        arrived(rx.at[n, 1], rx_recv.at[n, 1])
        s1[n, hz:nz, left] += rx[n, 1]
        send(s1.at[n, :, left], rb.at[n, 1], rb_send, rb_recv.at[n, 1], at_blk(z * nxc + left * 2 + core))

    def x_direct(h):
        c = slice(h * pc, (h + 1) * pc)
        n = 6 + h
        arrived(ra.at[n], ra_recv.at[n])
        s1[n] = (part[3, :, core, :, c] + ra[n]).reshape(nz, nx, NA, pc)
        for d in (2, 1, 3):
            p = (x + d) % nx
            send(s1.at[n, :, p], rd.at[h, d - 1], rd_send, rd_recv.at[h], at_blk(z * nxc + p * 2 + core))

    def z_stage(slot, h):
        n = slot * 2 + h
        if slot == 3:
            arrived(rd.at[h], rd_recv.at[h])
            s2[n] = s1[n, :, x] + rd[h, 0] + rd[h, 1] + rd[h, 2]
        else:
            for k in (0, 1):
                arrived(rb.at[n, k], rb_recv.at[n, k])
            s2[n] = s1[n, :, x] + rb[n, 0] + rb[n, 1]
        for d in order[::-1][:-1]:
            p = zpeer(d)
            send(s2.at[n, p], rc.at[n, d - 1], rc_send, rc_recv.at[n], at_blk(p * nxc + xc))

    def final(slot, h):
        n = slot * 2 + h
        arrived(rc.at[n], rc_recv.at[n])
        total = s2[n, z]
        for d in range(nz - 1):
            total = total + rc[n, d]
        up_date = total / den[n]
        for b in range(NB):
            upd_ref[slot_y[slot] * NB + b, :, h * hj:(h + 1) * hj] = up_date[:, b * hj:(b + 1) * hj]
        sq = jnp.sum(total * total, axis=0, keepdims=True)
        if pc < 128:
            sq = jnp.concatenate([sq, jnp.zeros((1, 128 - pc), F32)], axis=1)
        return sq

    def denominators():
        for copy in load_e:
            copy.wait()

        def pick(ref, at):
            lane = lax.broadcasted_iota(jnp.int32, ref.shape, 1)
            return jnp.sum(jnp.where(lane == at, ref[...], 0.0), axis=1, keepdims=True)

        mine_o = pick(occ_v, me)
        wide = (NA, va_v.shape[1])
        lane = lax.broadcasted_iota(jnp.int32, wide, 1)
        sub = lax.broadcasted_iota(jnp.int32, wide, 0)
        va = jnp.sum(
            jnp.where(lane == y * NA + sub, jnp.broadcast_to(va_v[...], wide), 0.0), axis=1, keepdims=True)
        for h in (0, 1):
            occ = jnp.concatenate([occ_v[:, h * hj:(h + 1) * hj]] * NB, axis=1)
            for slot in range(NY):
                vb = jnp.concatenate(
                    [jnp.broadcast_to(pick(vb_v, slot_y[slot] * NB + b), (1, hj)) for b in range(NB)], axis=1)
                den[slot * 2 + h] = ((mine_o + occ) - va) - vb

    def relay_stage(d):
        zs = (z + d) % nz
        arrived(a1.at[rows(zs * zrows, zrows)], z_recv.at[zs])
        second_stage(a1, zs)

    load_w.wait()
    prep_integrals(wv, 0)
    for d in order[1:3]:
        relay_stage(d)
    first = tb.at[rows(down * blk_rows, half)]
    arrived(first, ty_recv.at[0, 0])
    send(first, first, tf_send, tf_recv.at[0], at_y(up))
    second = tb.at[rows(up * blk_rows + half, half)]
    arrived(second, ty_recv.at[1, 1])
    send(second, second, tf_send, tf_recv.at[1], at_y(down))
    load_x.wait()
    prep_integrals(xv, 1)
    for d in order[3:]:
        relay_stage(d)
    denominators()
    load_t.wait()
    cycle_term(0)

    for q in range(nz):
        arrived(tt.at[rows(mine + q * zrows, zrows - ROWS)], c_recv.at[q])
        arrived(tt.at[rows(mine + q * zrows, ROWS)], c_loc.at[q])
        chunk = tt.at[rows(mine + q * zrows, zrows)]
        send(chunk, chunk, tty_send, tty_recv.at[0, q], at_y(up))
        send(chunk, chunk, tty_send, tty_recv.at[1, q], at_y(down))

    cross_term(0, 0)
    core_stage(0, 0)
    cross_term(0, 1)
    core_stage(0, 1)
    arrived(tb.at[rows(down * blk_rows + half, half)], ty_recv.at[0, 1])
    cycle_term(1)
    x_stage1(0, 0)
    x_stage1(0, 1)
    arrived(tb.at[rows(up * blk_rows, half)], ty_recv.at[1, 0])
    cycle_term(2)
    x_stage2(0, 0)
    x_stage2(0, 1)
    arrived(tb.at[rows(far * blk_rows, half)], tf_recv.at[0])
    arrived(tb.at[rows(far * blk_rows + half, half)], tf_recv.at[1])
    cycle_term(3)
    z_stage(0, 0)
    z_stage(0, 1)

    def near(h):
        for q in range(h * hz, (h + 1) * hz):
            for way, src_y in enumerate((down, up)):
                chunk = tt.at[rows(src_y * blk_rows + q * zrows, zrows)]
                arrived(chunk, tty_recv.at[way, q])
                if q % 2 == way:
                    send(chunk, chunk, ttf_send, ttf_recv.at[q], at_y((up, down)[way]))

    def distant(h):
        for q in range(h * hz, (h + 1) * hz):
            arrived(tt.at[rows(far * blk_rows + q * zrows, zrows)], ttf_recv.at[q])

    near(0)
    cross_term(1, 0)
    core_stage(1, 0)
    cross_term(2, 0)
    core_stage(2, 0)
    ss = final(0, 0)
    ss = ss + final(0, 1)
    x_stage1(1, 0)
    x_stage1(2, 0)
    near(1)
    x_stage2(1, 0)
    x_stage2(2, 0)
    cross_term(1, 1)
    core_stage(1, 1)
    cross_term(2, 1)
    core_stage(2, 1)
    x_stage1(1, 1)
    x_stage1(2, 1)
    z_stage(1, 0)
    z_stage(2, 0)
    distant(0)
    cross_term(3, 0)
    core_stage(3, 0)
    x_direct(0)
    distant(1)
    cross_term(3, 1)
    core_stage(3, 1)
    x_stage2(1, 1)
    x_stage2(2, 1)
    x_direct(1)
    ss = ss + final(1, 0)
    ss = ss + final(2, 0)
    z_stage(3, 0)
    z_stage(1, 1)
    z_stage(2, 1)
    z_stage(3, 1)
    ss = ss + final(3, 0)
    ss = ss + final(1, 1)
    ss = ss + final(2, 1)
    ss = ss + final(3, 1)

    def add_slots(ref, n):
        total = ref[0]
        for k in range(1, n):
            total = total + ref[k]
        return total

    ssz[z] = ss
    for d in order[::-1][:-1]:
        send(ssz.at[z], ssz.at[z], ss_send.at[0], ss_recv.at[0], at_blk(zpeer(d) * nxc + xc))
    arrived(ssz.at[pl.ds(0, nz - 1)], ss_recv.at[0])
    slot = y * nxc + xc
    ssp[slot] = add_slots(ssz, nz)
    peers = list(plane_peers())
    for peer in peers[::-1]:
        send(ssp.at[slot], ssp.at[slot], ss_send.at[1], ss_recv.at[1], peer)
    arrived(ssp.at[pl.ds(0, len(peers))], ss_recv.at[1])
    total = jnp.sum(add_slots(ssp, NY * nxc), keepdims=True)
    size = no * no * NA * NY * NB * NY
    rms_ref[...] = jnp.sqrt(total / size)

    arrived(tb.at[rows(0, 2 * blk_rows)], ty_send)
    arrived(tb.at[rows(0, blk_rows)], tf_send)
    arrived(a1.at[rows(0, (nz - 1) * zrows)], z_send)
    arrived(tt.at[rows(0, nz * (nxc - 1) * ROWS)], c_send)
    arrived(tt.at[rows(0, 2 * blk_rows)], tty_send)
    arrived(tt.at[rows(0, blk_rows)], ttf_send)
    arrived(ra, ra_send)
    arrived(rx, rx_send)
    arrived(rb, rb_send)
    arrived(rd, rd_send)
    arrived(rc, rc_send)
    arrived(ssz.at[pl.ds(0, nz - 1)], ss_send.at[0])
    arrived(ssp.at[pl.ds(0, len(peers))], ss_send.at[1])


def contractions(nz, nx, *args):
    nxc = nx * 2
    no = nz * nxc
    n = NB * no
    np = 2 * NY
    pc = n // 2
    dma = pltpu.SemaphoreType.DMA
    return pl.pallas_call(
        functools.partial(kernel, nz, nx),
        out_shape=(jax.ShapeDtypeStruct((NY * NB, NA, no), F32), jax.ShapeDtypeStruct((1, 1), F32)),
        in_specs=[pl.BlockSpec(memory_space=pl.ANY)] * 6,
        out_specs=(pl.BlockSpec(memory_space=pltpu.VMEM), pl.BlockSpec(memory_space=pltpu.VMEM)),
        scratch_shapes=[
            pltpu.VMEM((NY * no * ROWS + ROWS, 128), F32),
            pltpu.VMEM((NY * no * ROWS + ROWS, 128), F32),
            pltpu.VMEM((no * ROWS, 128), F32),
            pltpu.VMEM(((NA + 1) * no * CT, 128), F32),
            pltpu.VMEM(((NA + 1) * no * CT, 128), F32),
            pltpu.VMEM((1, no), F32),
            pltpu.VMEM((1, NA * NY), F32),
            pltpu.VMEM((1, NB * NY), F32),
            pltpu.VMEM((np, NA, pc), F32),
            pltpu.VMEM((NA * no, 2 * KT), BF16),
            pltpu.VMEM((n, 2 * KT), BF16),
            pltpu.VMEM((NY, nz * nx, 2, NA, n), F32),
            pltpu.VMEM((np, nz * nx, NA, pc), F32),
            pltpu.VMEM((np, nz, nx, NA, pc), F32),
            pltpu.VMEM((np - 2, 2, nz // 2, NA, pc), F32),
            pltpu.VMEM((np - 2, 2, nz, NA, pc), F32),
            pltpu.VMEM((2, 3, nz, NA, pc), F32),
            pltpu.VMEM((np, nz, NA, pc), F32),
            pltpu.VMEM((np, nz - 1, NA, pc), F32),
            pltpu.VMEM((nz, 1, 128), F32),
            pltpu.VMEM((NY * nxc, 1, 128), F32),
            dma((6,)),
            dma, dma((2, 2)), dma, dma((2,)),
            dma, dma((nz,)), dma, dma((nz,)), dma((nz,)),
            dma, dma((2, nz)), dma, dma((nz,)),
            dma, dma((np,)), dma, dma((np - 2, 2)), dma, dma((np - 2, 2)), dma, dma((2,)),
            dma, dma((np,)),
            dma((2,)), dma((2,)),
        ],
        compiler_params=pltpu.CompilerParams(collective_id=0, has_side_effects=True),
    )(*args)


def per_device(nz, nx, amplitudes, cycle_integrals, cross_integrals, occ_energy, vir_energy_a, vir_energy_b):
    no = nz * nx * 2
    t = amplitudes.reshape(no, NB, CT, 128).transpose(0, 2, 1, 3).reshape(no * ROWS, 128)
    w = cycle_integrals.reshape(NA * no * CT, 128)
    x = cross_integrals.reshape(NA * no * CT, 128)
    update, rms = contractions(
        nz, nx, t, w, x, occ_energy.reshape(1, -1), vir_energy_a.reshape(1, -1), vir_energy_b.reshape(1, -1))
    return update.transpose(1, 0, 2)[None], rms.reshape(())


def solution(mesh, nz=8, nx=4):
    return jax.shard_map(
        functools.partial(per_device, nz, nx),
        mesh=mesh,
        in_specs=(
            P("blk", None, "rep", None),
            P("rep", None, "blk", None),
            P("rep", None, "blk", None),
            P(),
            P(),
            P(),
        ),
        out_specs=(P("blk", "rep", None, None), P()),
        check_vma=False,
    )
```

```python
import functools

import jax
import jax.numpy as jnp
from jax import lax
from jax.experimental import pallas as pl
from jax.experimental.pallas import tpu as pltpu
from jax.sharding import PartitionSpec as P

MESH = pl.DeviceIdType.MESH
F32 = jnp.float32
BF16 = jnp.bfloat16
NY = 4
NB = 4
NA = 8
NC = 512
CT = NC // 128
ROWS = NB * CT
KT = 3 * NC


def ring_order(n):
    order = [0]
    for d in range(1, n // 2 + 1):
        order.append(d)
        if n - d != d:
            order.append(n - d)
    return order


def kernel(
    nz, nx,
    t_hbm, w_hbm, x_hbm, occ_hbm, va_hbm, vb_hbm, upd_ref, rms_ref,
    tb, tt, a1, wv, xv, occ_v, va_v, vb_v, den, wop, top, part, ra, s1, rx, rb, rd, s2, rc, ssz, ssp,
    load_sem, ty_send, ty_recv, tf_send, tf_recv, z_send, z_recv, c_send, c_recv, c_loc,
    tty_send, tty_recv, ttf_send, ttf_recv, ra_send, ra_recv, rx_send, rx_recv, rb_send, rb_recv, rd_send, rd_recv, rc_send, rc_recv,
    ss_send, ss_recv,
):
    nxc = nx * 2
    no = nz * nxc
    blk_rows = no * ROWS
    hj = no // 2
    pc = NB * hj
    me, y = lax.axis_index("blk"), lax.axis_index("rep")
    z, xc = me // nxc, me % nxc
    x, core = xc // 2, xc % 2
    up, down, far = (y + 1) % NY, (y + NY - 1) % NY, (y + 2) % NY
    right, left, across = (x + 1) % nx, (x + nx - 1) % nx, (x + 2) % nx
    slot_y = (y, down, up, far)
    order = ring_order(nz)

    def at_y(yy):
        return {"blk": me, "rep": yy}

    def at_blk(b):
        return {"blk": b, "rep": y}

    def zpeer(d):
        return (z + d) % nz

    def xcpeer(d):
        return (xc + d) % nxc

    def send(src, dst, ssem, rsem, dev):
        pltpu.make_async_remote_copy(
            src_ref=src, dst_ref=dst, send_sem=ssem, recv_sem=rsem, device_id=dev, device_id_type=MESH
        ).start()

    def arrived(ref, sem):
        pltpu.make_async_copy(ref, ref, sem).wait()

    def rows(start, n):
        return pl.ds(pl.multiple_of(start, ROWS), n)

    barrier = pltpu.get_barrier_semaphore()
    count = 0
    for d in range(1, nz):
        pl.semaphore_signal(barrier, inc=1, device_id=at_blk(zpeer(d) * nxc + xc), device_id_type=MESH)
        count += 1

    def plane_peers():
        for e in (1, NY - 1, 0, 2):
            for d in range(nxc):
                if d or e:
                    yield {"blk": z * nxc + xcpeer(d), "rep": (y + e) % NY}

    for peer in plane_peers():
        pl.semaphore_signal(barrier, inc=1, device_id=peer, device_id_type=MESH)
        count += 1
    pl.semaphore_wait(barrier, count)

    half = blk_rows // 2
    mine = y * blk_rows

    for h in (0, 1):
        send(t_hbm.at[rows(h * half, half)], tb.at[rows(mine + h * half, half)],
             ty_send, ty_recv.at[0, h], at_y(up))
        g = 1 - h
        send(t_hbm.at[rows(g * half, half)], tb.at[rows(mine + g * half, half)],
             ty_send, ty_recv.at[1, g], at_y(down))

    zrows = nxc * ROWS
    for d in order[1:]:
        zp = zpeer(d)
        send(t_hbm.at[rows(zp * zrows, zrows)], a1.at[rows(z * zrows, zrows)],
             z_send, z_recv.at[z], at_blk(zp * nxc + xc))

    def second_stage(src, zs):
        for d in range(1, nxc):
            p = xcpeer(d)
            send(src.at[rows(zs * zrows + p * ROWS, ROWS)], tt.at[rows(mine + zs * zrows + xc * ROWS, ROWS)],
                 c_send, c_recv.at[zs], at_blk(z * nxc + p))
        pltpu.make_async_copy(
            src.at[rows(zs * zrows + xc * ROWS, ROWS)], tt.at[rows(mine + zs * zrows + xc * ROWS, ROWS)],
            c_loc.at[zs]).start()

    second_stage(t_hbm, z)
    load_w = pltpu.make_async_copy(w_hbm, wv.at[pl.ds(0, NA * no * CT)], load_sem.at[0])
    load_x = pltpu.make_async_copy(x_hbm, xv.at[pl.ds(0, NA * no * CT)], load_sem.at[1])
    load_t = pltpu.make_async_copy(t_hbm, tb.at[rows(mine, blk_rows)], load_sem.at[2])
    load_w.start()
    load_x.start()
    load_t.start()
    load_e = [
        pltpu.make_async_copy(src, dst, load_sem.at[3 + k])
        for k, (src, dst) in enumerate(((occ_hbm, occ_v), (va_hbm, va_v), (vb_hbm, vb_v)))
    ]
    for copy in load_e:
        copy.start()

    def split(v):
        hi = v.astype(BF16)
        return hi, (v - hi.astype(F32)).astype(BF16)

    def prep_integrals(src, term):
        stride = no * CT

        def step(i2, carry):
            out = pl.ds(pl.multiple_of(i2 * 16, 16), 16)
            for ct in range(CT):
                v = jnp.concatenate(
                    [src[pl.ds((i2 * 2 + e) * CT + ct, NA, stride=stride), :] for e in range(2)], axis=0)
                hi, lo = split(v)
                base = term * KT + ct * 128
                wop[out, base:base + 128] = hi
                wop[out, base + NC:base + NC + 128] = lo
                wop[out, base + 2 * NC:base + 2 * NC + 128] = hi
            return carry

        lax.fori_loop(0, no // 2, step, 0)

    def prep_amplitudes(src, yb, term, h):
        def step(b, carry):
            out = pl.ds(pl.multiple_of(h * pc + b * hj, hj), hj)
            for ct in range(CT):
                v = src[pl.ds(yb * blk_rows + h * hj * ROWS + ct * NB + b, hj, stride=ROWS), :]
                hi, lo = split(v)
                base = term * KT + ct * 128
                top[out, base:base + 128] = hi
                top[out, base + NC:base + NC + 128] = hi
                top[out, base + 2 * NC:base + 2 * NC + 128] = lo
            return carry

        lax.fori_loop(0, NB, step, 0)

    def product(term, kk, r):
        cols = pl.ds(pl.multiple_of(term * KT + kk * NC, NC), NC)
        p = lax.dot_general(wop[:, cols], top[r, cols], (((1,), (1,)), ((), ())), preferred_element_type=F32)
        return p.reshape(nz * nx, 2, NA, p.shape[1])

    def cycle_term(slot):
        for h in (0, 1):
            prep_amplitudes(tb, slot_y[slot], 0, h)
        part[slot] = product(0, 0, slice(None))

        def step(kk, carry):
            part[slot] += product(0, kk, slice(None))
            return carry

        lax.fori_loop(1, KT // NC, step, 0)

    def cross_term(slot, h):
        prep_amplitudes(tt, slot_y[slot], 1, h)
        c = slice(h * pc, (h + 1) * pc)

        def step(kk, carry):
            part[slot, :, :, :, c] += product(1, kk, c)
            return carry

        lax.fori_loop(0, KT // NC, step, 0)

    def core_stage(slot, h):
        c = slice(h * pc, (h + 1) * pc)
        n = slot * 2 + h
        send(part.at[slot, :, 1 - core, :, c], ra.at[n], ra_send, ra_recv.at[n], at_blk(z * nxc + x * 2 + 1 - core))

    hz = nz // 2

    def x_stage1(slot, h):
        c = slice(h * pc, (h + 1) * pc)
        n = slot * 2 + h
        arrived(ra.at[n], ra_recv.at[n])
        s1[n] = (part[slot, :, core, :, c] + ra[n]).reshape(nz, nx, NA, pc)
        send(s1.at[n, 0:hz, across], rx.at[n, 0], rx_send, rx_recv.at[n, 0], at_blk(z * nxc + right * 2 + core))
        send(s1.at[n, hz:nz, across], rx.at[n, 1], rx_send, rx_recv.at[n, 1], at_blk(z * nxc + left * 2 + core))

    def x_stage2(slot, h):
        n = slot * 2 + h
        arrived(rx.at[n, 0], rx_recv.at[n, 0])
        s1[n, 0:hz, right] += rx[n, 0]
        send(s1.at[n, :, right], rb.at[n, 0], rb_send, rb_recv.at[n, 0], at_blk(z * nxc + right * 2 + core))
        arrived(rx.at[n, 1], rx_recv.at[n, 1])
        s1[n, hz:nz, left] += rx[n, 1]
        send(s1.at[n, :, left], rb.at[n, 1], rb_send, rb_recv.at[n, 1], at_blk(z * nxc + left * 2 + core))

    def x_direct(h):
        c = slice(h * pc, (h + 1) * pc)
        n = 6 + h
        arrived(ra.at[n], ra_recv.at[n])
        s1[n] = (part[3, :, core, :, c] + ra[n]).reshape(nz, nx, NA, pc)
        for d in (2, 1, 3):
            p = (x + d) % nx
            send(s1.at[n, :, p], rd.at[h, d - 1], rd_send, rd_recv.at[h], at_blk(z * nxc + p * 2 + core))

    def z_stage(slot, h):
        n = slot * 2 + h
        if slot == 3:
            arrived(rd.at[h], rd_recv.at[h])
            s2[n] = s1[n, :, x] + rd[h, 0] + rd[h, 1] + rd[h, 2]
        else:
            for k in (0, 1):
                arrived(rb.at[n, k], rb_recv.at[n, k])
            s2[n] = s1[n, :, x] + rb[n, 0] + rb[n, 1]
        for d in order[::-1][:-1]:
            p = zpeer(d)
            send(s2.at[n, p], rc.at[n, d - 1], rc_send, rc_recv.at[n], at_blk(p * nxc + xc))

    def final(slot, h):
        n = slot * 2 + h
        arrived(rc.at[n], rc_recv.at[n])
        total = s2[n, z]
        for d in range(nz - 1):
            total = total + rc[n, d]
        up_date = total / den[n]
        for b in range(NB):
            upd_ref[slot_y[slot] * NB + b, :, h * hj:(h + 1) * hj] = up_date[:, b * hj:(b + 1) * hj]
        sq = jnp.sum(total * total, axis=0, keepdims=True)
        if pc < 128:
            sq = jnp.concatenate([sq, jnp.zeros((1, 128 - pc), F32)], axis=1)
        return sq

    def denominators():
        for copy in load_e:
            copy.wait()

        def pick(ref, at):
            lane = lax.broadcasted_iota(jnp.int32, ref.shape, 1)
            return jnp.sum(jnp.where(lane == at, ref[...], 0.0), axis=1, keepdims=True)

        mine_o = pick(occ_v, me)
        wide = (NA, va_v.shape[1])
        lane = lax.broadcasted_iota(jnp.int32, wide, 1)
        sub = lax.broadcasted_iota(jnp.int32, wide, 0)
        va = jnp.sum(
            jnp.where(lane == y * NA + sub, jnp.broadcast_to(va_v[...], wide), 0.0), axis=1, keepdims=True)
        for h in (0, 1):
            occ = jnp.concatenate([occ_v[:, h * hj:(h + 1) * hj]] * NB, axis=1)
            for slot in range(NY):
                vb = jnp.concatenate(
                    [jnp.broadcast_to(pick(vb_v, slot_y[slot] * NB + b), (1, hj)) for b in range(NB)], axis=1)
                den[slot * 2 + h] = ((mine_o + occ) - va) - vb

    def relay_stage(d):
        zs = (z + d) % nz
        arrived(a1.at[rows(zs * zrows, zrows)], z_recv.at[zs])
        second_stage(a1, zs)

    load_w.wait()
    prep_integrals(wv, 0)
    for d in order[1:3]:
        relay_stage(d)
    first = tb.at[rows(down * blk_rows, half)]
    arrived(first, ty_recv.at[0, 0])
    send(first, first, tf_send, tf_recv.at[0], at_y(up))
    second = tb.at[rows(up * blk_rows + half, half)]
    arrived(second, ty_recv.at[1, 1])
    send(second, second, tf_send, tf_recv.at[1], at_y(down))
    load_x.wait()
    prep_integrals(xv, 1)
    for d in order[3:]:
        relay_stage(d)
    denominators()
    load_t.wait()
    cycle_term(0)

    for q in range(nz):
        arrived(tt.at[rows(mine + q * zrows, zrows - ROWS)], c_recv.at[q])
        arrived(tt.at[rows(mine + q * zrows, ROWS)], c_loc.at[q])
        chunk = tt.at[rows(mine + q * zrows, zrows)]
        send(chunk, chunk, tty_send, tty_recv.at[0, q], at_y(up))
        send(chunk, chunk, tty_send, tty_recv.at[1, q], at_y(down))

    cross_term(0, 0)
    core_stage(0, 0)
    cross_term(0, 1)
    core_stage(0, 1)
    arrived(tb.at[rows(down * blk_rows + half, half)], ty_recv.at[0, 1])
    cycle_term(1)
    x_stage1(0, 0)
    x_stage1(0, 1)
    arrived(tb.at[rows(up * blk_rows, half)], ty_recv.at[1, 0])
    cycle_term(2)
    x_stage2(0, 0)
    x_stage2(0, 1)
    arrived(tb.at[rows(far * blk_rows, half)], tf_recv.at[0])
    arrived(tb.at[rows(far * blk_rows + half, half)], tf_recv.at[1])
    cycle_term(3)

    def near(h):
        for q in range(h * hz, (h + 1) * hz):
            for way, src_y in enumerate((down, up)):
                chunk = tt.at[rows(src_y * blk_rows + q * zrows, zrows)]
                arrived(chunk, tty_recv.at[way, q])
                if q % 2 == way:
                    send(chunk, chunk, ttf_send, ttf_recv.at[q], at_y((up, down)[way]))

    def distant(h):
        for q in range(h * hz, (h + 1) * hz):
            arrived(tt.at[rows(far * blk_rows + q * zrows, zrows)], ttf_recv.at[q])

    near(0)
    cross_term(1, 0)
    core_stage(1, 0)
    cross_term(2, 0)
    core_stage(2, 0)
    z_stage(0, 0)
    z_stage(0, 1)
    x_stage1(1, 0)
    x_stage1(2, 0)
    near(1)
    cross_term(1, 1)
    core_stage(1, 1)
    cross_term(2, 1)
    core_stage(2, 1)
    x_stage2(1, 0)
    x_stage2(2, 0)
    x_stage1(1, 1)
    x_stage1(2, 1)
    distant(0)
    cross_term(3, 0)
    core_stage(3, 0)
    z_stage(1, 0)
    z_stage(2, 0)
    x_direct(0)
    distant(1)
    cross_term(3, 1)
    core_stage(3, 1)
    x_stage2(1, 1)
    x_stage2(2, 1)
    x_direct(1)
    z_stage(3, 0)
    z_stage(1, 1)
    z_stage(2, 1)
    z_stage(3, 1)
    ss = final(0, 0)
    ss = ss + final(0, 1)
    ss = ss + final(1, 0)
    ss = ss + final(2, 0)
    ss = ss + final(3, 0)
    ss = ss + final(1, 1)
    ss = ss + final(2, 1)
    ss = ss + final(3, 1)

    def add_slots(ref, n):
        total = ref[0]
        for k in range(1, n):
            total = total + ref[k]
        return total

    ssz[z] = ss
    for d in order[::-1][:-1]:
        send(ssz.at[z], ssz.at[z], ss_send.at[0], ss_recv.at[0], at_blk(zpeer(d) * nxc + xc))
    arrived(ssz.at[pl.ds(0, nz - 1)], ss_recv.at[0])
    slot = y * nxc + xc
    ssp[slot] = add_slots(ssz, nz)
    peers = list(plane_peers())
    for peer in peers[::-1]:
        send(ssp.at[slot], ssp.at[slot], ss_send.at[1], ss_recv.at[1], peer)
    arrived(ssp.at[pl.ds(0, len(peers))], ss_recv.at[1])
    total = jnp.sum(add_slots(ssp, NY * nxc), keepdims=True)
    size = no * no * NA * NY * NB * NY
    rms_ref[...] = jnp.sqrt(total / size)

    arrived(tb.at[rows(0, 2 * blk_rows)], ty_send)
    arrived(tb.at[rows(0, blk_rows)], tf_send)
    arrived(a1.at[rows(0, (nz - 1) * zrows)], z_send)
    arrived(tt.at[rows(0, nz * (nxc - 1) * ROWS)], c_send)
    arrived(tt.at[rows(0, 2 * blk_rows)], tty_send)
    arrived(tt.at[rows(0, blk_rows)], ttf_send)
    arrived(ra, ra_send)
    arrived(rx, rx_send)
    arrived(rb, rb_send)
    arrived(rd, rd_send)
    arrived(rc, rc_send)
    arrived(ssz.at[pl.ds(0, nz - 1)], ss_send.at[0])
    arrived(ssp.at[pl.ds(0, len(peers))], ss_send.at[1])


def contractions(nz, nx, *args):
    nxc = nx * 2
    no = nz * nxc
    n = NB * no
    np = 2 * NY
    pc = n // 2
    dma = pltpu.SemaphoreType.DMA
    return pl.pallas_call(
        functools.partial(kernel, nz, nx),
        out_shape=(jax.ShapeDtypeStruct((NY * NB, NA, no), F32), jax.ShapeDtypeStruct((1, 1), F32)),
        in_specs=[pl.BlockSpec(memory_space=pl.ANY)] * 6,
        out_specs=(pl.BlockSpec(memory_space=pltpu.VMEM), pl.BlockSpec(memory_space=pltpu.VMEM)),
        scratch_shapes=[
            pltpu.VMEM((NY * no * ROWS + ROWS, 128), F32),
            pltpu.VMEM((NY * no * ROWS + ROWS, 128), F32),
            pltpu.VMEM((no * ROWS, 128), F32),
            pltpu.VMEM(((NA + 1) * no * CT, 128), F32),
            pltpu.VMEM(((NA + 1) * no * CT, 128), F32),
            pltpu.VMEM((1, no), F32),
            pltpu.VMEM((1, NA * NY), F32),
            pltpu.VMEM((1, NB * NY), F32),
            pltpu.VMEM((np, NA, pc), F32),
            pltpu.VMEM((NA * no, 2 * KT), BF16),
            pltpu.VMEM((n, 2 * KT), BF16),
            pltpu.VMEM((NY, nz * nx, 2, NA, n), F32),
            pltpu.VMEM((np, nz * nx, NA, pc), F32),
            pltpu.VMEM((np, nz, nx, NA, pc), F32),
            pltpu.VMEM((np - 2, 2, nz // 2, NA, pc), F32),
            pltpu.VMEM((np - 2, 2, nz, NA, pc), F32),
            pltpu.VMEM((2, 3, nz, NA, pc), F32),
            pltpu.VMEM((np, nz, NA, pc), F32),
            pltpu.VMEM((np, nz - 1, NA, pc), F32),
            pltpu.VMEM((nz, 1, 128), F32),
            pltpu.VMEM((NY * nxc, 1, 128), F32),
            dma((6,)),
            dma, dma((2, 2)), dma, dma((2,)),
            dma, dma((nz,)), dma, dma((nz,)), dma((nz,)),
            dma, dma((2, nz)), dma, dma((nz,)),
            dma, dma((np,)), dma, dma((np - 2, 2)), dma, dma((np - 2, 2)), dma, dma((2,)),
            dma, dma((np,)),
            dma((2,)), dma((2,)),
        ],
        compiler_params=pltpu.CompilerParams(collective_id=0, has_side_effects=True),
    )(*args)


def per_device(nz, nx, amplitudes, cycle_integrals, cross_integrals, occ_energy, vir_energy_a, vir_energy_b):
    no = nz * nx * 2
    t = amplitudes.reshape(no, NB, CT, 128).transpose(0, 2, 1, 3).reshape(no * ROWS, 128)
    w = cycle_integrals.reshape(NA * no * CT, 128)
    x = cross_integrals.reshape(NA * no * CT, 128)
    update, rms = contractions(
        nz, nx, t, w, x, occ_energy.reshape(1, -1), vir_energy_a.reshape(1, -1), vir_energy_b.reshape(1, -1))
    return update.transpose(1, 0, 2)[None], rms.reshape(())


def solution(mesh, nz=8, nx=4):
    return jax.shard_map(
        functools.partial(per_device, nz, nx),
        mesh=mesh,
        in_specs=(
            P("blk", None, "rep", None),
            P("rep", None, "blk", None),
            P("rep", None, "blk", None),
            P(),
            P(),
            P(),
        ),
        out_specs=(P("blk", "rep", None, None), P()),
        check_vma=False,
    )
```

```python
import functools

import jax
import jax.numpy as jnp
from jax import lax
from jax.experimental import pallas as pl
from jax.experimental.pallas import tpu as pltpu
from jax.sharding import PartitionSpec as P

MESH = pl.DeviceIdType.MESH
F32 = jnp.float32
BF16 = jnp.bfloat16
NY = 4
NB = 4
NA = 8
NC = 512
CT = NC // 128
ROWS = NB * CT
KT = 3 * NC


def ring_order(n):
    order = [0]
    for d in range(1, n // 2 + 1):
        order.append(d)
        if n - d != d:
            order.append(n - d)
    return order


def kernel(
    nz, nx,
    t_hbm, w_hbm, x_hbm, occ_hbm, va_hbm, vb_hbm, upd_ref, rms_ref,
    tb, tt, a1, a2, wv, xv, occ_v, va_v, vb_v, den, wop, top, part, ra, s1, rx, rb, rd, s2, rc, ssz, ssp,
    load_sem, ty_send, ty_recv, tf_send, tf_recv, z_send, z_recv, c_send, c_recv, c_loc,
    tty_send, tty_recv, ttf_send, ttf_recv, ra_send, ra_recv, rx_send, rx_recv, rb_send, rb_recv, rd_send, rd_recv, rc_send, rc_recv,
    ss_send, ss_recv, e_send, e_recv, e_loc, g_send, g_recv, f_send, f_recv, f_loc,
):
    nxc = nx * 2
    no = nz * nxc
    blk_rows = no * ROWS
    hj = no // 2
    pc = NB * hj
    me, y = lax.axis_index("blk"), lax.axis_index("rep")
    z, xc = me // nxc, me % nxc
    x, core = xc // 2, xc % 2
    up, down, far = (y + 1) % NY, (y + NY - 1) % NY, (y + 2) % NY
    right, left, across = (x + 1) % nx, (x + nx - 1) % nx, (x + 2) % nx
    slot_y = (y, down, up, far)
    order = ring_order(nz)
    close = order[:3]

    def at_y(yy):
        return {"blk": me, "rep": yy}

    def at_blk(b):
        return {"blk": b, "rep": y}

    def zpeer(d):
        return (z + d) % nz

    def xcpeer(d):
        return (xc + d) % nxc

    def send(src, dst, ssem, rsem, dev):
        pltpu.make_async_remote_copy(
            src_ref=src, dst_ref=dst, send_sem=ssem, recv_sem=rsem, device_id=dev, device_id_type=MESH
        ).start()

    def arrived(ref, sem):
        pltpu.make_async_copy(ref, ref, sem).wait()

    def rows(start, n):
        return pl.ds(pl.multiple_of(start, ROWS), n)

    barrier = pltpu.get_barrier_semaphore()
    count = 0
    for d in range(1, nz):
        pl.semaphore_signal(barrier, inc=1, device_id=at_blk(zpeer(d) * nxc + xc), device_id_type=MESH)
        count += 1

    def plane_peers():
        for e in (1, NY - 1, 0, 2):
            for d in range(nxc):
                if d or e:
                    yield {"blk": z * nxc + xcpeer(d), "rep": (y + e) % NY}

    for peer in plane_peers():
        pl.semaphore_signal(barrier, inc=1, device_id=peer, device_id_type=MESH)
        count += 1
    pl.semaphore_wait(barrier, count)

    half = blk_rows // 2
    mine = y * blk_rows

    for h in (0, 1):
        send(t_hbm.at[rows(h * half, half)], tb.at[rows(mine + h * half, half)],
             ty_send, ty_recv.at[0, h], at_y(up))
        g = 1 - h
        send(t_hbm.at[rows(g * half, half)], tb.at[rows(mine + g * half, half)],
             ty_send, ty_recv.at[1, g], at_y(down))

    zrows = nxc * ROWS
    for d in order[1:]:
        zp = zpeer(d)
        send(t_hbm.at[rows(zp * zrows, zrows)], a1.at[rows(z * zrows, zrows)],
             z_send, z_recv.at[z], at_blk(zp * nxc + xc))

    def second_stage(src, base, yb, zs, ssem, rsem, lsem):
        to = yb * blk_rows + zs * zrows + xc * ROWS
        for d in range(1, nxc):
            p = xcpeer(d)
            send(src.at[rows(base + p * ROWS, ROWS)], tt.at[rows(to, ROWS)], ssem, rsem, at_blk(z * nxc + p))
        pltpu.make_async_copy(src.at[rows(base + xc * ROWS, ROWS)], tt.at[rows(to, ROWS)], lsem).start()

    def second_arrived(yb, zs, rsem, lsem):
        arrived(tt.at[rows(yb * blk_rows + zs * zrows, zrows - ROWS)], rsem)
        arrived(tt.at[rows(yb * blk_rows + zs * zrows, ROWS)], lsem)

    second_stage(t_hbm, z * zrows, y, z, c_send, c_recv.at[z], c_loc.at[z])
    load_w = pltpu.make_async_copy(w_hbm, wv.at[pl.ds(0, NA * no * CT)], load_sem.at[0])
    load_x = pltpu.make_async_copy(x_hbm, xv.at[pl.ds(0, NA * no * CT)], load_sem.at[1])
    load_t = pltpu.make_async_copy(t_hbm, tb.at[rows(mine, blk_rows)], load_sem.at[2])
    load_w.start()
    load_x.start()
    load_t.start()
    load_e = [
        pltpu.make_async_copy(src, dst, load_sem.at[3 + k])
        for k, (src, dst) in enumerate(((occ_hbm, occ_v), (va_hbm, va_v), (vb_hbm, vb_v)))
    ]
    for copy in load_e:
        copy.start()

    def split(v):
        hi = v.astype(BF16)
        return hi, (v - hi.astype(F32)).astype(BF16)

    def prep_integrals(src, term):
        stride = no * CT

        def step(i2, carry):
            out = pl.ds(pl.multiple_of(i2 * 16, 16), 16)
            for ct in range(CT):
                v = jnp.concatenate(
                    [src[pl.ds((i2 * 2 + e) * CT + ct, NA, stride=stride), :] for e in range(2)], axis=0)
                hi, lo = split(v)
                base = term * KT + ct * 128
                wop[out, base:base + 128] = hi
                wop[out, base + NC:base + NC + 128] = lo
                wop[out, base + 2 * NC:base + 2 * NC + 128] = hi
            return carry

        lax.fori_loop(0, no // 2, step, 0)

    def prep_amplitudes(src, yb, term, h):
        def step(b, carry):
            out = pl.ds(pl.multiple_of(h * pc + b * hj, hj), hj)
            for ct in range(CT):
                v = src[pl.ds(yb * blk_rows + h * hj * ROWS + ct * NB + b, hj, stride=ROWS), :]
                hi, lo = split(v)
                base = term * KT + ct * 128
                top[out, base:base + 128] = hi
                top[out, base + NC:base + NC + 128] = hi
                top[out, base + 2 * NC:base + 2 * NC + 128] = lo
            return carry

        lax.fori_loop(0, NB, step, 0)

    def product(term, kk, r):
        cols = pl.ds(pl.multiple_of(term * KT + kk * NC, NC), NC)
        p = lax.dot_general(wop[:, cols], top[r, cols], (((1,), (1,)), ((), ())), preferred_element_type=F32)
        return p.reshape(nz * nx, 2, NA, p.shape[1])

    def cycle_term(slot):
        for h in (0, 1):
            prep_amplitudes(tb, slot_y[slot], 0, h)
        part[slot] = product(0, 0, slice(None))

        def step(kk, carry):
            part[slot] += product(0, kk, slice(None))
            return carry

        lax.fori_loop(1, KT // NC, step, 0)

    def cross_term(slot, h):
        prep_amplitudes(tt, slot_y[slot], 1, h)
        c = slice(h * pc, (h + 1) * pc)

        def step(kk, carry):
            part[slot, :, :, :, c] += product(1, kk, c)
            return carry

        lax.fori_loop(0, KT // NC, step, 0)

    def core_stage(slot, h):
        c = slice(h * pc, (h + 1) * pc)
        n = slot * 2 + h
        send(part.at[slot, :, 1 - core, :, c], ra.at[n], ra_send, ra_recv.at[n], at_blk(z * nxc + x * 2 + 1 - core))

    hz = nz // 2

    def x_stage1(slot, h):
        c = slice(h * pc, (h + 1) * pc)
        n = slot * 2 + h
        arrived(ra.at[n], ra_recv.at[n])
        s1[n] = (part[slot, :, core, :, c] + ra[n]).reshape(nz, nx, NA, pc)
        send(s1.at[n, 0:hz, across], rx.at[n, 0], rx_send, rx_recv.at[n, 0], at_blk(z * nxc + right * 2 + core))
        send(s1.at[n, hz:nz, across], rx.at[n, 1], rx_send, rx_recv.at[n, 1], at_blk(z * nxc + left * 2 + core))

    def x_stage2(slot, h):
        n = slot * 2 + h
        arrived(rx.at[n, 0], rx_recv.at[n, 0])
        s1[n, 0:hz, right] += rx[n, 0]
        send(s1.at[n, :, right], rb.at[n, 0], rb_send, rb_recv.at[n, 0], at_blk(z * nxc + right * 2 + core))
        arrived(rx.at[n, 1], rx_recv.at[n, 1])
        s1[n, hz:nz, left] += rx[n, 1]
        send(s1.at[n, :, left], rb.at[n, 1], rb_send, rb_recv.at[n, 1], at_blk(z * nxc + left * 2 + core))

    def x_direct(h):
        c = slice(h * pc, (h + 1) * pc)
        n = 6 + h
        arrived(ra.at[n], ra_recv.at[n])
        s1[n] = (part[3, :, core, :, c] + ra[n]).reshape(nz, nx, NA, pc)
        for d in (2, 1, 3):
            p = (x + d) % nx
            send(s1.at[n, :, p], rd.at[h, d - 1], rd_send, rd_recv.at[h], at_blk(z * nxc + p * 2 + core))

    def z_stage(slot, h):
        n = slot * 2 + h
        if slot == 3:
            arrived(rd.at[h], rd_recv.at[h])
            s2[n] = s1[n, :, x] + rd[h, 0] + rd[h, 1] + rd[h, 2]
        else:
            for k in (0, 1):
                arrived(rb.at[n, k], rb_recv.at[n, k])
            s2[n] = s1[n, :, x] + rb[n, 0] + rb[n, 1]
        for d in order[::-1][:-1]:
            p = zpeer(d)
            send(s2.at[n, p], rc.at[n, d - 1], rc_send, rc_recv.at[n], at_blk(p * nxc + xc))

    def final(slot, h):
        n = slot * 2 + h
        arrived(rc.at[n], rc_recv.at[n])
        total = s2[n, z]
        for d in range(nz - 1):
            total = total + rc[n, d]
        up_date = total / den[n]
        for b in range(NB):
            upd_ref[slot_y[slot] * NB + b, :, h * hj:(h + 1) * hj] = up_date[:, b * hj:(b + 1) * hj]
        sq = jnp.sum(total * total, axis=0, keepdims=True)
        if pc < 128:
            sq = jnp.concatenate([sq, jnp.zeros((1, 128 - pc), F32)], axis=1)
        return sq

    def denominators():
        for copy in load_e:
            copy.wait()

        def pick(ref, at):
            lane = lax.broadcasted_iota(jnp.int32, ref.shape, 1)
            return jnp.sum(jnp.where(lane == at, ref[...], 0.0), axis=1, keepdims=True)

        mine_o = pick(occ_v, me)
        wide = (NA, va_v.shape[1])
        lane = lax.broadcasted_iota(jnp.int32, wide, 1)
        sub = lax.broadcasted_iota(jnp.int32, wide, 0)
        va = jnp.sum(
            jnp.where(lane == y * NA + sub, jnp.broadcast_to(va_v[...], wide), 0.0), axis=1, keepdims=True)
        for h in (0, 1):
            occ = jnp.concatenate([occ_v[:, h * hj:(h + 1) * hj]] * NB, axis=1)
            for slot in range(NY):
                vb = jnp.concatenate(
                    [jnp.broadcast_to(pick(vb_v, slot_y[slot] * NB + b), (1, hj)) for b in range(NB)], axis=1)
                den[slot * 2 + h] = ((mine_o + occ) - va) - vb

    def relay_stage(d):
        zs = (z + d) % nz
        arrived(a1.at[rows(zs * zrows, zrows)], z_recv.at[zs])
        second_stage(a1, zs * zrows, y, zs, c_send, c_recv.at[zs], c_loc.at[zs])

    load_w.wait()
    prep_integrals(wv, 0)
    for d in order[1:3]:
        relay_stage(d)
    first = tb.at[rows(down * blk_rows, half)]
    arrived(first, ty_recv.at[0, 0])
    send(first, first, tf_send, tf_recv.at[0], at_y(up))
    second = tb.at[rows(up * blk_rows + half, half)]
    arrived(second, ty_recv.at[1, 1])
    send(second, second, tf_send, tf_recv.at[1], at_y(down))
    load_x.wait()
    prep_integrals(xv, 1)
    for d in order[3:]:
        relay_stage(d)
    denominators()
    load_t.wait()
    cycle_term(0)

    for q in range(nz):
        second_arrived(y, q, c_recv.at[q], c_loc.at[q])

        @pl.when(z != q)
        def _():
            chunk = tt.at[rows(mine + q * zrows, zrows)]
            send(chunk, chunk, tty_send, tty_recv.at[0, q], at_y(up))
            send(chunk, chunk, tty_send, tty_recv.at[1, q], at_y(down))

    arrived(tb.at[rows(down * blk_rows + half, half)], ty_recv.at[0, 1])
    second_stage(tb, down * blk_rows + z * zrows, down, z, e_send, e_recv.at[0], e_loc.at[0])
    arrived(tb.at[rows(up * blk_rows, half)], ty_recv.at[1, 0])
    second_stage(tb, up * blk_rows + z * zrows, up, z, e_send, e_recv.at[1], e_loc.at[1])
    cross_term(0, 0)
    core_stage(0, 0)
    cross_term(0, 1)
    core_stage(0, 1)
    arrived(tb.at[rows(far * blk_rows, half)], tf_recv.at[0])
    arrived(tb.at[rows(far * blk_rows + half, half)], tf_recv.at[1])
    for d in close[1:]:
        zp = zpeer(d)
        send(tb.at[rows(far * blk_rows + zp * zrows, zrows)], a2.at[rows(z * zrows, zrows)],
             g_send, g_recv.at[z], at_blk(zp * nxc + xc))
    second_stage(tb, far * blk_rows + z * zrows, far, z, f_send, f_recv.at[z], f_loc.at[z])
    cycle_term(1)
    x_stage1(0, 0)
    x_stage1(0, 1)
    cycle_term(2)
    x_stage2(0, 0)
    x_stage2(0, 1)
    cycle_term(3)

    def is_close(q):
        apart = (q + nz - z) % nz
        out = apart == close[0]
        for d in close[1:]:
            out = jnp.logical_or(out, apart == d)
        return out

    def near(h):
        for q in range(h * hz, (h + 1) * hz):
            @pl.when(z != q)
            def _():
                for way, src_y in enumerate((down, up)):
                    arrived(tt.at[rows(src_y * blk_rows + q * zrows, zrows)], tty_recv.at[way, q])

            @pl.when(jnp.logical_not(is_close(q)))
            def _():
                src_y, dst_y = ((down, up), (up, down))[q % 2]
                chunk = tt.at[rows(src_y * blk_rows + q * zrows, zrows)]
                send(chunk, chunk, ttf_send, ttf_recv.at[q], at_y(dst_y))

            @pl.when(z == q)
            def _():
                second_arrived(down, q, e_recv.at[0], e_loc.at[0])
                second_arrived(up, q, e_recv.at[1], e_loc.at[1])

    def relay_far(d):
        zs = (z + d) % nz
        arrived(a2.at[rows(zs * zrows, zrows)], g_recv.at[zs])
        second_stage(a2, zs * zrows, far, zs, f_send, f_recv.at[zs], f_loc.at[zs])

    def distant(h):
        for q in range(h * hz, (h + 1) * hz):
            @pl.when(is_close(q))
            def _():
                second_arrived(far, q, f_recv.at[q], f_loc.at[q])

            @pl.when(jnp.logical_not(is_close(q)))
            def _():
                arrived(tt.at[rows(far * blk_rows + q * zrows, zrows)], ttf_recv.at[q])

    near(0)
    for d in close[1:3]:
        relay_far(d)
    cross_term(1, 0)
    core_stage(1, 0)
    cross_term(2, 0)
    core_stage(2, 0)
    for d in close[3:]:
        relay_far(d)
    z_stage(0, 0)
    z_stage(0, 1)
    x_stage1(1, 0)
    x_stage1(2, 0)
    near(1)
    cross_term(1, 1)
    core_stage(1, 1)
    cross_term(2, 1)
    core_stage(2, 1)
    x_stage2(1, 0)
    x_stage2(2, 0)
    x_stage1(1, 1)
    x_stage1(2, 1)
    distant(0)
    cross_term(3, 0)
    core_stage(3, 0)
    z_stage(1, 0)
    z_stage(2, 0)
    x_direct(0)
    distant(1)
    cross_term(3, 1)
    core_stage(3, 1)
    x_stage2(1, 1)
    x_stage2(2, 1)
    x_direct(1)
    z_stage(3, 0)
    z_stage(1, 1)
    z_stage(2, 1)
    z_stage(3, 1)
    ss = final(0, 0)
    ss = ss + final(0, 1)
    ss = ss + final(1, 0)
    ss = ss + final(2, 0)
    ss = ss + final(3, 0)
    ss = ss + final(1, 1)
    ss = ss + final(2, 1)
    ss = ss + final(3, 1)

    def add_slots(ref, n):
        total = ref[0]
        for k in range(1, n):
            total = total + ref[k]
        return total

    ssz[z] = ss
    for d in order[::-1][:-1]:
        send(ssz.at[z], ssz.at[z], ss_send.at[0], ss_recv.at[0], at_blk(zpeer(d) * nxc + xc))
    arrived(ssz.at[pl.ds(0, nz - 1)], ss_recv.at[0])
    slot = y * nxc + xc
    ssp[slot] = add_slots(ssz, nz)
    peers = list(plane_peers())
    for peer in peers[::-1]:
        send(ssp.at[slot], ssp.at[slot], ss_send.at[1], ss_recv.at[1], peer)
    arrived(ssp.at[pl.ds(0, len(peers))], ss_recv.at[1])
    total = jnp.sum(add_slots(ssp, NY * nxc), keepdims=True)
    size = no * no * NA * NY * NB * NY
    rms_ref[...] = jnp.sqrt(total / size)

    arrived(tb.at[rows(0, 2 * blk_rows)], ty_send)
    arrived(tb.at[rows(0, blk_rows)], tf_send)
    arrived(a1.at[rows(0, (nz - 1) * zrows)], z_send)
    arrived(tt.at[rows(0, nz * (nxc - 1) * ROWS)], c_send)
    arrived(tt.at[rows(0, 2 * (nz - 1) * zrows)], tty_send)
    if nz > len(close):
        arrived(tt.at[rows(0, (nz - len(close)) * zrows)], ttf_send)
    arrived(tt.at[rows(0, 2 * (nxc - 1) * ROWS)], e_send)
    arrived(tt.at[rows(0, len(close) * (nxc - 1) * ROWS)], f_send)
    arrived(a2.at[rows(0, (len(close) - 1) * zrows)], g_send)
    arrived(ra, ra_send)
    arrived(rx, rx_send)
    arrived(rb, rb_send)
    arrived(rd, rd_send)
    arrived(rc, rc_send)
    arrived(ssz.at[pl.ds(0, nz - 1)], ss_send.at[0])
    arrived(ssp.at[pl.ds(0, len(peers))], ss_send.at[1])


def contractions(nz, nx, *args):
    nxc = nx * 2
    no = nz * nxc
    n = NB * no
    np = 2 * NY
    pc = n // 2
    dma = pltpu.SemaphoreType.DMA
    return pl.pallas_call(
        functools.partial(kernel, nz, nx),
        out_shape=(jax.ShapeDtypeStruct((NY * NB, NA, no), F32), jax.ShapeDtypeStruct((1, 1), F32)),
        in_specs=[pl.BlockSpec(memory_space=pl.ANY)] * 6,
        out_specs=(pl.BlockSpec(memory_space=pltpu.VMEM), pl.BlockSpec(memory_space=pltpu.VMEM)),
        scratch_shapes=[
            pltpu.VMEM((NY * no * ROWS + ROWS, 128), F32),
            pltpu.VMEM((NY * no * ROWS + ROWS, 128), F32),
            pltpu.VMEM((no * ROWS, 128), F32),
            pltpu.VMEM((no * ROWS, 128), F32),
            pltpu.VMEM(((NA + 1) * no * CT, 128), F32),
            pltpu.VMEM(((NA + 1) * no * CT, 128), F32),
            pltpu.VMEM((1, no), F32),
            pltpu.VMEM((1, NA * NY), F32),
            pltpu.VMEM((1, NB * NY), F32),
            pltpu.VMEM((np, NA, pc), F32),
            pltpu.VMEM((NA * no, 2 * KT), BF16),
            pltpu.VMEM((n, 2 * KT), BF16),
            pltpu.VMEM((NY, nz * nx, 2, NA, n), F32),
            pltpu.VMEM((np, nz * nx, NA, pc), F32),
            pltpu.VMEM((np, nz, nx, NA, pc), F32),
            pltpu.VMEM((np - 2, 2, nz // 2, NA, pc), F32),
            pltpu.VMEM((np - 2, 2, nz, NA, pc), F32),
            pltpu.VMEM((2, 3, nz, NA, pc), F32),
            pltpu.VMEM((np, nz, NA, pc), F32),
            pltpu.VMEM((np, nz - 1, NA, pc), F32),
            pltpu.VMEM((nz, 1, 128), F32),
            pltpu.VMEM((NY * nxc, 1, 128), F32),
            dma((6,)),
            dma, dma((2, 2)), dma, dma((2,)),
            dma, dma((nz,)), dma, dma((nz,)), dma((nz,)),
            dma, dma((2, nz)), dma, dma((nz,)),
            dma, dma((np,)), dma, dma((np - 2, 2)), dma, dma((np - 2, 2)), dma, dma((2,)),
            dma, dma((np,)),
            dma((2,)), dma((2,)),
            dma, dma((2,)), dma((2,)), dma, dma((nz,)), dma, dma((nz,)), dma((nz,)),
        ],
        compiler_params=pltpu.CompilerParams(collective_id=0, has_side_effects=True),
    )(*args)


def per_device(nz, nx, amplitudes, cycle_integrals, cross_integrals, occ_energy, vir_energy_a, vir_energy_b):
    no = nz * nx * 2
    t = amplitudes.reshape(no, NB, CT, 128).transpose(0, 2, 1, 3).reshape(no * ROWS, 128)
    w = cycle_integrals.reshape(NA * no * CT, 128)
    x = cross_integrals.reshape(NA * no * CT, 128)
    update, rms = contractions(
        nz, nx, t, w, x, occ_energy.reshape(1, -1), vir_energy_a.reshape(1, -1), vir_energy_b.reshape(1, -1))
    return update.transpose(1, 0, 2)[None], rms.reshape(())


def solution(mesh, nz=8, nx=4):
    return jax.shard_map(
        functools.partial(per_device, nz, nx),
        mesh=mesh,
        in_specs=(
            P("blk", None, "rep", None),
            P("rep", None, "blk", None),
            P("rep", None, "blk", None),
            P(),
            P(),
            P(),
        ),
        out_specs=(P("blk", "rep", None, None), P()),
        check_vma=False,
    )
```

```python
import functools

import jax
import jax.numpy as jnp
from jax import lax
from jax.experimental import pallas as pl
from jax.experimental.pallas import tpu as pltpu
from jax.sharding import PartitionSpec as P

MESH = pl.DeviceIdType.MESH
F32 = jnp.float32
BF16 = jnp.bfloat16
NY = 4
NB = 4
NA = 8
NC = 512
CT = NC // 128
ROWS = NB * CT
KT = 3 * NC


def ring_order(n):
    order = [0]
    for d in range(1, n // 2 + 1):
        order.append(d)
        if n - d != d:
            order.append(n - d)
    return order


def kernel(
    nz, nx,
    t_hbm, w_hbm, x_hbm, occ_hbm, va_hbm, vb_hbm, upd_ref, rms_ref,
    tb, tt, a1, a2, wv, xv, occ_v, va_v, vb_v, den, wop, top, part, ra, s1, rx, rb, rd, s2, rc, ssz, ssp,
    load_sem, ty_send, ty_recv, tf_send, tf_recv, z_send, z_recv, c_send, c_recv, c_loc,
    tty_send, tty_recv, ttf_send, ttf_recv, ra_send, ra_recv, rx_send, rx_recv, rb_send, rb_recv, rd_send, rd_recv, rc_send, rc_recv,
    ss_send, ss_recv, e_send, e_recv, e_loc, g_send, g_recv, f_send, f_recv, f_loc,
):
    nxc = nx * 2
    no = nz * nxc
    blk_rows = no * ROWS
    hj = no // 2
    pc = NB * hj
    me, y = lax.axis_index("blk"), lax.axis_index("rep")
    z, xc = me // nxc, me % nxc
    x, core = xc // 2, xc % 2
    up, down, far = (y + 1) % NY, (y + NY - 1) % NY, (y + 2) % NY
    right, left, across = (x + 1) % nx, (x + nx - 1) % nx, (x + 2) % nx
    slot_y = (y, down, up, far)
    order = ring_order(nz)
    close = order[:3]

    def at_y(yy):
        return {"blk": me, "rep": yy}

    def at_blk(b):
        return {"blk": b, "rep": y}

    def zpeer(d):
        return (z + d) % nz

    def xcpeer(d):
        return (xc + d) % nxc

    def send(src, dst, ssem, rsem, dev):
        pltpu.make_async_remote_copy(
            src_ref=src, dst_ref=dst, send_sem=ssem, recv_sem=rsem, device_id=dev, device_id_type=MESH
        ).start()

    def arrived(ref, sem):
        pltpu.make_async_copy(ref, ref, sem).wait()

    def rows(start, n):
        return pl.ds(pl.multiple_of(start, ROWS), n)

    barrier = pltpu.get_barrier_semaphore()
    count = 0
    for d in range(1, nz):
        pl.semaphore_signal(barrier, inc=1, device_id=at_blk(zpeer(d) * nxc + xc), device_id_type=MESH)
        count += 1

    def plane_peers():
        for e in (1, NY - 1, 0, 2):
            for d in range(nxc):
                if d or e:
                    yield {"blk": z * nxc + xcpeer(d), "rep": (y + e) % NY}

    for peer in plane_peers():
        pl.semaphore_signal(barrier, inc=1, device_id=peer, device_id_type=MESH)
        count += 1
    pl.semaphore_wait(barrier, count)

    half = blk_rows // 2
    mine = y * blk_rows

    for h in (0, 1):
        send(t_hbm.at[rows(h * half, half)], tb.at[rows(mine + h * half, half)],
             ty_send, ty_recv.at[0, h], at_y(up))
        g = 1 - h
        send(t_hbm.at[rows(g * half, half)], tb.at[rows(mine + g * half, half)],
             ty_send, ty_recv.at[1, g], at_y(down))

    zrows = nxc * ROWS
    for d in order[1:]:
        zp = zpeer(d)
        send(t_hbm.at[rows(zp * zrows, zrows)], a1.at[rows(z * zrows, zrows)],
             z_send, z_recv.at[z], at_blk(zp * nxc + xc))

    def second_stage(src, base, yb, zs, ssem, rsem, lsem):
        to = yb * blk_rows + zs * zrows + xc * ROWS
        for d in range(1, nxc):
            p = xcpeer(d)
            send(src.at[rows(base + p * ROWS, ROWS)], tt.at[rows(to, ROWS)], ssem, rsem, at_blk(z * nxc + p))
        pltpu.make_async_copy(src.at[rows(base + xc * ROWS, ROWS)], tt.at[rows(to, ROWS)], lsem).start()

    def second_arrived(yb, zs, rsem, lsem):
        arrived(tt.at[rows(yb * blk_rows + zs * zrows, zrows - ROWS)], rsem)
        arrived(tt.at[rows(yb * blk_rows + zs * zrows, ROWS)], lsem)

    second_stage(t_hbm, z * zrows, y, z, c_send, c_recv.at[z], c_loc.at[z])
    load_w = pltpu.make_async_copy(w_hbm, wv.at[pl.ds(0, NA * no * CT)], load_sem.at[0])
    load_x = pltpu.make_async_copy(x_hbm, xv.at[pl.ds(0, NA * no * CT)], load_sem.at[1])
    load_t = pltpu.make_async_copy(t_hbm, tb.at[rows(mine, blk_rows)], load_sem.at[2])
    load_w.start()
    load_x.start()
    load_t.start()
    load_e = [
        pltpu.make_async_copy(src, dst, load_sem.at[3 + k])
        for k, (src, dst) in enumerate(((occ_hbm, occ_v), (va_hbm, va_v), (vb_hbm, vb_v)))
    ]
    for copy in load_e:
        copy.start()

    def split(v):
        hi = v.astype(BF16)
        return hi, (v - hi.astype(F32)).astype(BF16)

    def prep_integrals(src, term):
        stride = no * CT

        def step(i2, carry):
            out = pl.ds(pl.multiple_of(i2 * 16, 16), 16)
            for ct in range(CT):
                v = jnp.concatenate(
                    [src[pl.ds((i2 * 2 + e) * CT + ct, NA, stride=stride), :] for e in range(2)], axis=0)
                hi, lo = split(v)
                base = term * KT + ct * 128
                wop[out, base:base + 128] = hi
                wop[out, base + NC:base + NC + 128] = lo
                wop[out, base + 2 * NC:base + 2 * NC + 128] = hi
            return carry

        lax.fori_loop(0, no // 2, step, 0)

    def prep_amplitudes(src, yb, term, h):
        def step(b, carry):
            out = pl.ds(pl.multiple_of(h * pc + b * hj, hj), hj)
            for ct in range(CT):
                v = src[pl.ds(yb * blk_rows + h * hj * ROWS + ct * NB + b, hj, stride=ROWS), :]
                hi, lo = split(v)
                base = term * KT + ct * 128
                top[out, base:base + 128] = hi
                top[out, base + NC:base + NC + 128] = hi
                top[out, base + 2 * NC:base + 2 * NC + 128] = lo
            return carry

        lax.fori_loop(0, NB, step, 0)

    def product(term, kk, r):
        cols = pl.ds(pl.multiple_of(term * KT + kk * NC, NC), NC)
        p = lax.dot_general(wop[:, cols], top[r, cols], (((1,), (1,)), ((), ())), preferred_element_type=F32)
        return p.reshape(nz * nx, 2, NA, p.shape[1])

    def cycle_term(slot):
        for h in (0, 1):
            prep_amplitudes(tb, slot_y[slot], 0, h)
        part[slot] = product(0, 0, slice(None))

        def step(kk, carry):
            part[slot] += product(0, kk, slice(None))
            return carry

        lax.fori_loop(1, KT // NC, step, 0)

    def cross_term(slot, h):
        prep_amplitudes(tt, slot_y[slot], 1, h)
        c = slice(h * pc, (h + 1) * pc)

        def step(kk, carry):
            part[slot, :, :, :, c] += product(1, kk, c)
            return carry

        lax.fori_loop(0, KT // NC, step, 0)

    def core_stage(slot, h):
        c = slice(h * pc, (h + 1) * pc)
        n = slot * 2 + h
        send(part.at[slot, :, 1 - core, :, c], ra.at[n], ra_send, ra_recv.at[n], at_blk(z * nxc + x * 2 + 1 - core))

    hz = nz // 2

    def x_stage1(slot, h):
        c = slice(h * pc, (h + 1) * pc)
        n = slot * 2 + h
        arrived(ra.at[n], ra_recv.at[n])
        s1[n] = (part[slot, :, core, :, c] + ra[n]).reshape(nz, nx, NA, pc)
        send(s1.at[n, 0:hz, across], rx.at[n, 0], rx_send, rx_recv.at[n, 0], at_blk(z * nxc + right * 2 + core))
        send(s1.at[n, hz:nz, across], rx.at[n, 1], rx_send, rx_recv.at[n, 1], at_blk(z * nxc + left * 2 + core))

    def x_stage2(slot, h):
        n = slot * 2 + h
        arrived(rx.at[n, 0], rx_recv.at[n, 0])
        s1[n, 0:hz, right] += rx[n, 0]
        send(s1.at[n, :, right], rb.at[n, 0], rb_send, rb_recv.at[n, 0], at_blk(z * nxc + right * 2 + core))
        arrived(rx.at[n, 1], rx_recv.at[n, 1])
        s1[n, hz:nz, left] += rx[n, 1]
        send(s1.at[n, :, left], rb.at[n, 1], rb_send, rb_recv.at[n, 1], at_blk(z * nxc + left * 2 + core))

    def x_direct(h):
        c = slice(h * pc, (h + 1) * pc)
        n = 6 + h
        arrived(ra.at[n], ra_recv.at[n])
        s1[n] = (part[3, :, core, :, c] + ra[n]).reshape(nz, nx, NA, pc)
        for d in (2, 1, 3):
            p = (x + d) % nx
            send(s1.at[n, :, p], rd.at[h, d - 1], rd_send, rd_recv.at[h], at_blk(z * nxc + p * 2 + core))

    def z_stage(slot, h):
        n = slot * 2 + h
        if slot == 3:
            arrived(rd.at[h], rd_recv.at[h])
            s2[n] = s1[n, :, x] + rd[h, 0] + rd[h, 1] + rd[h, 2]
        else:
            for k in (0, 1):
                arrived(rb.at[n, k], rb_recv.at[n, k])
            s2[n] = s1[n, :, x] + rb[n, 0] + rb[n, 1]
        for d in order[::-1][:-1]:
            p = zpeer(d)
            send(s2.at[n, p], rc.at[n, d - 1], rc_send, rc_recv.at[n], at_blk(p * nxc + xc))

    def final(slot, h):
        n = slot * 2 + h
        arrived(rc.at[n], rc_recv.at[n])
        total = s2[n, z]
        for d in range(nz - 1):
            total = total + rc[n, d]
        up_date = total / den[n]
        for b in range(NB):
            upd_ref[slot_y[slot] * NB + b, :, h * hj:(h + 1) * hj] = up_date[:, b * hj:(b + 1) * hj]
        sq = jnp.sum(total * total, axis=0, keepdims=True)
        if pc < 128:
            sq = jnp.concatenate([sq, jnp.zeros((1, 128 - pc), F32)], axis=1)
        return sq

    def denominators():
        for copy in load_e:
            copy.wait()

        def pick(ref, at):
            lane = lax.broadcasted_iota(jnp.int32, ref.shape, 1)
            return jnp.sum(jnp.where(lane == at, ref[...], 0.0), axis=1, keepdims=True)

        mine_o = pick(occ_v, me)
        wide = (NA, va_v.shape[1])
        lane = lax.broadcasted_iota(jnp.int32, wide, 1)
        sub = lax.broadcasted_iota(jnp.int32, wide, 0)
        va = jnp.sum(
            jnp.where(lane == y * NA + sub, jnp.broadcast_to(va_v[...], wide), 0.0), axis=1, keepdims=True)
        for h in (0, 1):
            occ = jnp.concatenate([occ_v[:, h * hj:(h + 1) * hj]] * NB, axis=1)
            for slot in range(NY):
                vb = jnp.concatenate(
                    [jnp.broadcast_to(pick(vb_v, slot_y[slot] * NB + b), (1, hj)) for b in range(NB)], axis=1)
                den[slot * 2 + h] = ((mine_o + occ) - va) - vb

    def relay_stage(d):
        zs = (z + d) % nz
        arrived(a1.at[rows(zs * zrows, zrows)], z_recv.at[zs])
        second_stage(a1, zs * zrows, y, zs, c_send, c_recv.at[zs], c_loc.at[zs])

    load_w.wait()
    prep_integrals(wv, 0)
    for d in order[1:3]:
        relay_stage(d)
    first = tb.at[rows(down * blk_rows, half)]
    arrived(first, ty_recv.at[0, 0])
    send(first, first, tf_send, tf_recv.at[0], at_y(up))
    second = tb.at[rows(up * blk_rows + half, half)]
    arrived(second, ty_recv.at[1, 1])
    send(second, second, tf_send, tf_recv.at[1], at_y(down))
    load_x.wait()
    prep_integrals(xv, 1)
    for d in order[3:]:
        relay_stage(d)
    denominators()
    load_t.wait()
    cycle_term(0)

    for q in range(nz):
        second_arrived(y, q, c_recv.at[q], c_loc.at[q])

        @pl.when(z != q)
        def _():
            chunk = tt.at[rows(mine + q * zrows, zrows)]
            send(chunk, chunk, tty_send, tty_recv.at[0, q], at_y(up))
            send(chunk, chunk, tty_send, tty_recv.at[1, q], at_y(down))

    arrived(tb.at[rows(down * blk_rows + half, half)], ty_recv.at[0, 1])
    second_stage(tb, down * blk_rows + z * zrows, down, z, e_send, e_recv.at[0], e_loc.at[0])
    arrived(tb.at[rows(up * blk_rows, half)], ty_recv.at[1, 0])
    second_stage(tb, up * blk_rows + z * zrows, up, z, e_send, e_recv.at[1], e_loc.at[1])
    cross_term(0, 0)
    core_stage(0, 0)
    cross_term(0, 1)
    core_stage(0, 1)
    arrived(tb.at[rows(far * blk_rows, half)], tf_recv.at[0])
    arrived(tb.at[rows(far * blk_rows + half, half)], tf_recv.at[1])
    for d in close[1:]:
        zp = zpeer(d)
        send(tb.at[rows(far * blk_rows + zp * zrows, zrows)], a2.at[rows(z * zrows, zrows)],
             g_send, g_recv.at[z], at_blk(zp * nxc + xc))
    second_stage(tb, far * blk_rows + z * zrows, far, z, f_send, f_recv.at[z], f_loc.at[z])
    cycle_term(1)
    x_stage1(0, 0)
    x_stage1(0, 1)
    cycle_term(2)
    x_stage2(0, 0)
    x_stage2(0, 1)
    cycle_term(3)

    def is_close(q):
        apart = (q + nz - z) % nz
        out = apart == close[0]
        for d in close[1:]:
            out = jnp.logical_or(out, apart == d)
        return out

    def near(h):
        for q in range(h * hz, (h + 1) * hz):
            @pl.when(z != q)
            def _():
                for way, src_y in enumerate((down, up)):
                    arrived(tt.at[rows(src_y * blk_rows + q * zrows, zrows)], tty_recv.at[way, q])

            @pl.when(jnp.logical_not(is_close(q)))
            def _():
                src_y, dst_y = ((down, up), (up, down))[q % 2]
                chunk = tt.at[rows(src_y * blk_rows + q * zrows, zrows)]
                send(chunk, chunk, ttf_send, ttf_recv.at[q], at_y(dst_y))

            @pl.when(z == q)
            def _():
                second_arrived(down, q, e_recv.at[0], e_loc.at[0])
                second_arrived(up, q, e_recv.at[1], e_loc.at[1])

    def relay_far(d):
        zs = (z + d) % nz
        arrived(a2.at[rows(zs * zrows, zrows)], g_recv.at[zs])
        second_stage(a2, zs * zrows, far, zs, f_send, f_recv.at[zs], f_loc.at[zs])

    def distant(h):
        for q in range(h * hz, (h + 1) * hz):
            @pl.when(is_close(q))
            def _():
                second_arrived(far, q, f_recv.at[q], f_loc.at[q])

            @pl.when(jnp.logical_not(is_close(q)))
            def _():
                arrived(tt.at[rows(far * blk_rows + q * zrows, zrows)], ttf_recv.at[q])

    near(0)
    for d in close[1:3]:
        relay_far(d)
    cross_term(1, 0)
    core_stage(1, 0)
    cross_term(2, 0)
    core_stage(2, 0)
    for d in close[3:]:
        relay_far(d)
    z_stage(0, 0)
    z_stage(0, 1)
    x_stage1(1, 0)
    x_stage1(2, 0)
    near(1)
    cross_term(1, 1)
    core_stage(1, 1)
    cross_term(2, 1)
    core_stage(2, 1)
    x_stage2(1, 0)
    x_stage2(2, 0)
    x_stage1(1, 1)
    x_stage1(2, 1)
    distant(0)
    cross_term(3, 0)
    core_stage(3, 0)
    z_stage(1, 0)
    z_stage(2, 0)
    x_direct(0)
    x_stage2(1, 1)
    x_stage2(2, 1)
    distant(1)
    cross_term(3, 1)
    core_stage(3, 1)
    x_direct(1)
    z_stage(3, 0)
    z_stage(1, 1)
    z_stage(2, 1)
    z_stage(3, 1)
    ss = final(0, 0)
    ss = ss + final(0, 1)
    ss = ss + final(1, 0)
    ss = ss + final(2, 0)
    ss = ss + final(3, 0)
    ss = ss + final(1, 1)
    ss = ss + final(2, 1)
    ss = ss + final(3, 1)

    def add_slots(ref, n):
        total = ref[0]
        for k in range(1, n):
            total = total + ref[k]
        return total

    ssz[z] = ss
    for d in order[::-1][:-1]:
        send(ssz.at[z], ssz.at[z], ss_send.at[0], ss_recv.at[0], at_blk(zpeer(d) * nxc + xc))
    arrived(ssz.at[pl.ds(0, nz - 1)], ss_recv.at[0])
    slot = y * nxc + xc
    ssp[slot] = add_slots(ssz, nz)
    peers = list(plane_peers())
    for peer in peers[::-1]:
        send(ssp.at[slot], ssp.at[slot], ss_send.at[1], ss_recv.at[1], peer)
    arrived(ssp.at[pl.ds(0, len(peers))], ss_recv.at[1])
    total = jnp.sum(add_slots(ssp, NY * nxc), keepdims=True)
    size = no * no * NA * NY * NB * NY
    rms_ref[...] = jnp.sqrt(total / size)

    arrived(tb.at[rows(0, 2 * blk_rows)], ty_send)
    arrived(tb.at[rows(0, blk_rows)], tf_send)
    arrived(a1.at[rows(0, (nz - 1) * zrows)], z_send)
    arrived(tt.at[rows(0, nz * (nxc - 1) * ROWS)], c_send)
    arrived(tt.at[rows(0, 2 * (nz - 1) * zrows)], tty_send)
    if nz > len(close):
        arrived(tt.at[rows(0, (nz - len(close)) * zrows)], ttf_send)
    arrived(tt.at[rows(0, 2 * (nxc - 1) * ROWS)], e_send)
    arrived(tt.at[rows(0, len(close) * (nxc - 1) * ROWS)], f_send)
    arrived(a2.at[rows(0, (len(close) - 1) * zrows)], g_send)
    arrived(ra, ra_send)
    arrived(rx, rx_send)
    arrived(rb, rb_send)
    arrived(rd, rd_send)
    arrived(rc, rc_send)
    arrived(ssz.at[pl.ds(0, nz - 1)], ss_send.at[0])
    arrived(ssp.at[pl.ds(0, len(peers))], ss_send.at[1])


def contractions(nz, nx, *args):
    nxc = nx * 2
    no = nz * nxc
    n = NB * no
    np = 2 * NY
    pc = n // 2
    dma = pltpu.SemaphoreType.DMA
    return pl.pallas_call(
        functools.partial(kernel, nz, nx),
        out_shape=(jax.ShapeDtypeStruct((NY * NB, NA, no), F32), jax.ShapeDtypeStruct((1, 1), F32)),
        in_specs=[pl.BlockSpec(memory_space=pl.ANY)] * 6,
        out_specs=(pl.BlockSpec(memory_space=pltpu.VMEM), pl.BlockSpec(memory_space=pltpu.VMEM)),
        scratch_shapes=[
            pltpu.VMEM((NY * no * ROWS + ROWS, 128), F32),
            pltpu.VMEM((NY * no * ROWS + ROWS, 128), F32),
            pltpu.VMEM((no * ROWS, 128), F32),
            pltpu.VMEM((no * ROWS, 128), F32),
            pltpu.VMEM(((NA + 1) * no * CT, 128), F32),
            pltpu.VMEM(((NA + 1) * no * CT, 128), F32),
            pltpu.VMEM((1, no), F32),
            pltpu.VMEM((1, NA * NY), F32),
            pltpu.VMEM((1, NB * NY), F32),
            pltpu.VMEM((np, NA, pc), F32),
            pltpu.VMEM((NA * no, 2 * KT), BF16),
            pltpu.VMEM((n, 2 * KT), BF16),
            pltpu.VMEM((NY, nz * nx, 2, NA, n), F32),
            pltpu.VMEM((np, nz * nx, NA, pc), F32),
            pltpu.VMEM((np, nz, nx, NA, pc), F32),
            pltpu.VMEM((np - 2, 2, nz // 2, NA, pc), F32),
            pltpu.VMEM((np - 2, 2, nz, NA, pc), F32),
            pltpu.VMEM((2, 3, nz, NA, pc), F32),
            pltpu.VMEM((np, nz, NA, pc), F32),
            pltpu.VMEM((np, nz - 1, NA, pc), F32),
            pltpu.VMEM((nz, 1, 128), F32),
            pltpu.VMEM((NY * nxc, 1, 128), F32),
            dma((6,)),
            dma, dma((2, 2)), dma, dma((2,)),
            dma, dma((nz,)), dma, dma((nz,)), dma((nz,)),
            dma, dma((2, nz)), dma, dma((nz,)),
            dma, dma((np,)), dma, dma((np - 2, 2)), dma, dma((np - 2, 2)), dma, dma((2,)),
            dma, dma((np,)),
            dma((2,)), dma((2,)),
            dma, dma((2,)), dma((2,)), dma, dma((nz,)), dma, dma((nz,)), dma((nz,)),
        ],
        compiler_params=pltpu.CompilerParams(collective_id=0, has_side_effects=True),
    )(*args)


def per_device(nz, nx, amplitudes, cycle_integrals, cross_integrals, occ_energy, vir_energy_a, vir_energy_b):
    no = nz * nx * 2
    t = amplitudes.reshape(no, NB, CT, 128).transpose(0, 2, 1, 3).reshape(no * ROWS, 128)
    w = cycle_integrals.reshape(NA * no * CT, 128)
    x = cross_integrals.reshape(NA * no * CT, 128)
    update, rms = contractions(
        nz, nx, t, w, x, occ_energy.reshape(1, -1), vir_energy_a.reshape(1, -1), vir_energy_b.reshape(1, -1))
    return update.transpose(1, 0, 2)[None], rms.reshape(())


def solution(mesh, nz=8, nx=4):
    return jax.shard_map(
        functools.partial(per_device, nz, nx),
        mesh=mesh,
        in_specs=(
            P("blk", None, "rep", None),
            P("rep", None, "blk", None),
            P("rep", None, "blk", None),
            P(),
            P(),
            P(),
        ),
        out_specs=(P("blk", "rep", None, None), P()),
        check_vma=False,
    )
```
